128 devices in a mesh: section: 4 (over x), dev: 32 (over y, z, core).
Axes of the slice: x: 4, y: 4, z: 4, core: 2. Of those that a mesh axis runs over, the one named last changes fastest.
Arguments:
- hidden: bfloat16 [1024, 2048], P('dev'), may hold values from -8 to 8
- lengths: int32 [1024], P('dev'), may hold values from 1 to 256, as said below
- attn_gain: float32 [2048], replicated, may hold values from 0.1 to 1.9
- w_query: bfloat16 [2048, 3072], P(None, 'section'), may hold values from -0.125 to 0.125
- w_latent: bfloat16 [2048, 512], replicated, may hold values from -0.125 to 0.125
- latent_gain: float32 [512], replicated, may hold values from 0.1 to 1.9
- w_rope_key: bfloat16 [64, 2048], replicated, may hold values from -0.125 to 0.125
- w_key_up: bfloat16 [16, 512, 128], P('section'), may hold values from -0.5 to 0.5
- w_value_up: bfloat16 [16, 512, 128], P('section'), may hold values from -0.25 to 0.25
- w_out: bfloat16 [2048, 2048], P('section'), may hold values from -0.125 to 0.125
- latent_cache: bfloat16 [1024, 256, 512], P('dev'), may hold values from -6 to 6
- rope_cache: bfloat16 [1024, 64, 256], P('dev'), may hold values from -1200 to 1200
- ffn_gain: float32 [2048], replicated, may hold values from 0.1 to 1.9
- expert_ids: int32 [1024, 6], P('dev'), may hold values from 0 to 63, all different within a row; in each aligned block of 8 rows (0 to 7, 8 to 15, ...) at most 2 rows name the same one
- route_weights: float32 [1024, 6], P('dev'), may hold values from 0.05 to 0.5
- w_gate_up: bfloat16 [64, 2, 1408, 2048], P('dev', None, 'section'), may hold values from -0.125 to 0.125
- w_down: bfloat16 [64, 1408, 2048], P('dev', 'section'), may hold values from -0.15625 to 0.15625
Outputs:
- layer_out: bfloat16 [1024, 2048], P('dev')
The draws below stay inside these ranges and needn't reach their ends.
Inputs may be any that keep to these rules, and one draw needn't show every extreme that they name: `lengths`: every aligned block of 32 rows holds a row of length 256. `expert_ids`: each row names 6 different experts. In every aligned block of 8 rows no expert is named by more than 2 rows, and some block has an expert named by exactly 2.
All inputs are finite; a program needn't handle non-finite values.
Results may differ from the reference program's by a relative error of at most 0.011.
Values may be sent and summed in bfloat16 or wider, within the bound.
No kernel may reach another device: no remote copies, remote signals or barrier semaphores. Data moves between devices by JAX's collectives and lax.ppermute only.
A program may use at most 128 MiB of HBM per device.

```python
import math
import jax
import jax.numpy as jnp
import numpy as np
from jax import lax

D = 2048
HEADS = 16
NOPE = 128
ROPE = 64
LATENT = 512
VHEAD = 128
FF = 1408
EXPERTS = 64
TOPK = 6
ROW_DEV = 32
LEN = 256
MOST = 2
ROWS = 1024
ROW_Q = 8


def draw_hidden(key, part):
    base_key, row_key, column_key = jax.random.split(jax.random.fold_in(key, 11), 3)
    row_scale = jnp.exp(jax.random.uniform(row_key, (ROWS, 1), jnp.float32, math.log(0.2), math.log(2.0)))
    column_scale = jnp.exp(jax.random.uniform(column_key, (1, D), jnp.float32, math.log(0.3), math.log(3.0)))
    values = jax.random.normal(base_key, (ROWS, D), jnp.float32)
    return jnp.clip(values * row_scale * column_scale, -8.0, 8.0).astype(jnp.bfloat16)


def draw_lengths(key, part):
    length_key, pick_key = jax.random.split(jax.random.fold_in(key, 23))
    values = jax.random.randint(length_key, (ROWS,), 1, LEN + 1, dtype=jnp.int32)
    chosen = jax.random.randint(pick_key, (ROWS // ROW_DEV,), 0, ROW_DEV, dtype=jnp.int32)
    positions = jnp.arange(ROWS, dtype=jnp.int32)
    full_row = positions % ROW_DEV == chosen[positions // ROW_DEV]
    return jnp.where(full_row, LEN, values).astype(jnp.int32)


def draw_rope_cache(key, part):
    base_key = jax.random.fold_in(jax.random.fold_in(key, 37), 0)
    values = jnp.clip(jax.random.normal(base_key, (ROWS, ROPE, LEN), jnp.float32), -6.0, 6.0)
    return jnp.clip(values, -1200.0, 1200.0).astype(jnp.bfloat16)


def steps_of(rng, extent, cuts, low, top_value):
    level = 1.0
    for dim, blocks in cuts:
        draws = jax.random.uniform(jax.random.fold_in(jax.random.fold_in(rng, 6), dim), (blocks,), jnp.float32, low / len(cuts), top_value / len(cuts))
        level = level * jnp.repeat(jnp.exp(draws), extent[dim] // blocks).reshape((-1,) + (1,) * (len(extent) - 1 - dim))
    return level


def routed_block(stream_key, own, number, rows, number_of, top, limit, lean):
    ranking = jax.random.permutation(stream_key, number_of)
    heavy_load, usual = load_shares(number_of, rows * top, limit, lean, True), load_shares(number_of, rows * top, limit, lean, False)
    places = jnp.arange(number_of)

    def named(sizes, turn):
        used = int((sizes > 0).sum())
        fixed = max(1, used // 4)
        passed = fixed + (places - fixed + turn * (used - fixed)) % max(1, number_of - fixed)
        return jnp.zeros((number_of,), jnp.int32).at[ranking[jnp.where(places < fixed, places, passed)]].set(jnp.asarray(sizes, jnp.int32))

    sizes = jnp.where(number % 4 == 0, named(heavy_load, number // 4), named(usual, number - number // 4 - 1))
    mixed = jax.random.permutation(jax.random.fold_in(own, 3), number_of)
    donor, taker = mixed[0:number_of // 2 * 2:2], mixed[1:number_of // 2 * 2:2]
    slack = jnp.minimum(sizes[donor] - 1, limit - sizes[taker]) // 2
    slack = jnp.where((donor == ranking[0]) | (taker == ranking[0]) | (sizes[taker] == 0), 0, jnp.maximum(slack, 0))
    passed = jax.random.randint(jax.random.fold_in(own, 4), (number_of // 2,), 0, 1 << 20) % (slack + 1)
    sizes = sizes.at[donor].add(-passed).at[taker].add(passed)
    items = jnp.searchsorted(jnp.cumsum(sizes), jnp.arange(rows * top), side="right").astype(jnp.int32)
    grid = items.reshape(top, rows).T
    grid = grid[jax.random.permutation(jax.random.fold_in(own, 1), rows)]
    turn = jax.random.randint(jax.random.fold_in(own, 2), (rows, 1), 0, top)
    return jnp.take_along_axis(grid, (jnp.arange(top)[None, :] + turn) % top, axis=1)


def load_shares(amount, total, bound, lean, full):
    weights = [(1 << 20) // math.isqrt(rank ** lean) + 1 for rank in range(1, amount + 1)]
    largest = bound if full else min(bound, max(-(-total // amount), total * weights[0] // sum(weights)))
    least = 1 if total - largest >= amount - 1 else 0
    holding, spare = [largest] + [least] * (amount - 1), total - largest - least * (amount - 1)
    while spare > 0:
        free = [i for i in range(1, amount) if holding[i] < largest] or [i for i in range(1, amount) if holding[i] < bound]
        mass, budget = sum([weights[i] for i in free]), spare
        for i in free:
            more = min(bound - holding[i], max(1, budget * weights[i] // mass), spare)
            holding[i] = holding[i] + more
            spare = spare - more
    return np.array(holding)


def gaussian(stream_key, extent, deviation, reach, cuts=(), held_as=jnp.bfloat16):
    array = deviation * jax.random.normal(stream_key, extent, jnp.float32)
    if cuts:
        array = array * steps_of(stream_key, extent, cuts, -0.22, 0.18)
    return jnp.clip(array, -reach, reach).astype(held_as)


def setup_inputs(seed: int = 0) -> dict:
    splits = jax.random.split(jax.random.key(seed), 18)
    hidden = draw_hidden(jax.random.fold_in(splits[17], 71), 0)
    lengths = draw_lengths(jax.random.fold_in(splits[17], 71), 0)
    attn_gain = jnp.clip(1.0 + 0.18 * jax.random.normal(splits[2], (D,), jnp.float32), 0.1, 1.9)
    w_query = gaussian(splits[3], (D, HEADS * (NOPE + ROPE)), D ** -0.5, 0.125, ((1, 4),))
    w_latent = gaussian(splits[4], (D, LATENT), D ** -0.5, 0.125)
    latent_gain = jnp.clip(1.0 + 0.18 * jax.random.normal(splits[5], (LATENT,), jnp.float32), 0.1, 1.9)
    w_rope_key = gaussian(splits[6], (ROPE, D), D ** -0.5, 0.125)
    w_key_up = gaussian(splits[7], (HEADS, LATENT, NOPE), NOPE ** -0.5, 0.5, ((0, 4),))
    w_value_up = gaussian(splits[8], (HEADS, LATENT, VHEAD), LATENT ** -0.5, 0.25, ((0, 4),))
    w_out = gaussian(splits[9], (HEADS * VHEAD, D), (HEADS * VHEAD) ** -0.5, 0.125, ((0, 4),))
    latent_cache = gaussian(splits[10], (ROWS, LEN, LATENT), 1.0, 6.0, ((0, 32),))
    rope_cache = draw_rope_cache(jax.random.fold_in(splits[17], 71), 0)
    ffn_gain = jnp.clip(1.0 + 0.18 * jax.random.normal(splits[12], (D,), jnp.float32), 0.1, 1.9)
    expert_ids_keys = jax.random.split(jax.random.fold_in(splits[13], 1), ROWS // ROW_Q)
    expert_ids_turns = jax.random.permutation(jax.random.fold_in(splits[13], 3), ROWS // ROW_Q)
    expert_ids = jax.vmap(lambda own, number: routed_block(jax.random.fold_in(splits[13], 2), own, number, ROW_Q, EXPERTS, TOPK, MOST, 2))(expert_ids_keys, expert_ids_turns).reshape((ROWS, TOPK))
    route_weights = jnp.clip(jnp.exp(math.log(0.5) - 2.3025851 * jax.random.uniform(splits[14], (ROWS, TOPK), jnp.float32) ** steps_of(splits[14], (ROWS, TOPK), ((0, 32),), -0.2, 0.2)), 0.05, 0.5)
    w_gate_up = gaussian(splits[15], (EXPERTS, 2, FF, D), D ** -0.5, 0.125, ((0, 32), (2, 4)))
    w_down = gaussian(splits[16], (EXPERTS, FF, D), FF ** -0.5, 0.15625, ((0, 32), (1, 4)))
    return dict(hidden=hidden, lengths=lengths, attn_gain=attn_gain, w_query=w_query, w_latent=w_latent, latent_gain=latent_gain, w_rope_key=w_rope_key, w_key_up=w_key_up, w_value_up=w_value_up, w_out=w_out, latent_cache=latent_cache, rope_cache=rope_cache, ffn_gain=ffn_gain, expert_ids=expert_ids, route_weights=route_weights, w_gate_up=w_gate_up, w_down=w_down)


epsilon = 1e-06
far_below = -1e+30

def rms_norm(values, norm_gain):
    mean_square = lax.optimization_barrier(jnp.mean(values * values, axis=-1, keepdims=True))
    return values * lax.rsqrt(mean_square + epsilon) * norm_gain

def rotary(values, positions):
    half_width = values.shape[-1] // 2
    step_index = jnp.arange(half_width, dtype=jnp.float32)
    frequency = jnp.exp(-jnp.log(10000.0) * step_index / half_width)
    angles = positions.astype(jnp.float32)[:, None] * frequency[None, :]
    if values.ndim == 3:
        angles = angles[:, None, :]
    cosine = jnp.cos(angles)
    sine_part = jnp.sin(angles)
    first_half = values[..., :half_width]
    second = values[..., half_width:]
    return jnp.concatenate([first_half * cosine - second * sine_part, second * cosine + first_half * sine_part], axis=-1)

def slot_targets(expert_ids, block_rows):
    row_count, top_count = expert_ids.shape
    blocks = row_count // block_rows
    flat_ids = expert_ids.reshape(blocks, block_rows * top_count)
    onehot = (flat_ids[:, :, None] == jnp.arange(EXPERTS, dtype=jnp.int32)[None, None, :]).astype(jnp.int32)
    earlier = jnp.cumsum(onehot, axis=1) - onehot
    rank_in = lax.optimization_barrier(jnp.sum(earlier * onehot, axis=2))
    capacity = blocks * MOST
    target = flat_ids * capacity + jnp.arange(blocks, dtype=jnp.int32)[:, None] * MOST + rank_in
    return (target.reshape(row_count, top_count).astype(jnp.int32), capacity)

def attend(query_latent, query_rope, latent_new, key_new, latent_cache, rope_cache, lengths, score_scale):
    scores = jnp.einsum('rhl,rtl->rht', query_latent.astype(jnp.float32), latent_cache.astype(jnp.float32))
    scores = scores + jnp.einsum('rhp,rpt->rht', query_rope.astype(jnp.float32), rope_cache.astype(jnp.float32))
    scores = scores * score_scale
    self_score = jnp.einsum('rhl,rl->rh', query_latent.astype(jnp.float32), latent_new.astype(jnp.float32))
    self_score = (self_score + jnp.einsum('rhp,rp->rh', query_rope.astype(jnp.float32), key_new.astype(jnp.float32))) * score_scale
    places = jnp.arange(latent_cache.shape[1], dtype=jnp.int32)
    valid_mask = places[None, None, :] < lengths[:, None, None]
    masked = jnp.where(valid_mask, scores, far_below)
    peak_score = jnp.maximum(lax.optimization_barrier(jnp.max(masked, axis=2)), self_score)
    weights = jnp.where(valid_mask, jnp.exp(masked - peak_score[:, :, None]), 0.0)
    self_weight = jnp.exp(self_score - peak_score)
    totals = lax.optimization_barrier(jnp.sum(weights, axis=2)) + self_weight
    prob_cache = (weights / totals[:, :, None]).astype(jnp.bfloat16)
    prob_self = (self_weight / totals).astype(jnp.bfloat16)
    mixed = jnp.einsum('rht,rtl->rhl', prob_cache.astype(jnp.float32), latent_cache.astype(jnp.float32))
    mixed = mixed + prob_self.astype(jnp.float32)[:, :, None] * latent_new.astype(jnp.float32)[:, None, :]
    return mixed.astype(jnp.bfloat16)

def reference(hidden, lengths, attn_gain, w_query, w_latent, latent_gain, w_rope_key, w_key_up, w_value_up, w_out, latent_cache, rope_cache, ffn_gain, expert_ids, route_weights, w_gate_up, w_down):
    normed = rms_norm(hidden.astype(jnp.float32), attn_gain).astype(jnp.bfloat16)
    queries = jnp.dot(normed, w_query, preferred_element_type=jnp.float32).astype(jnp.bfloat16)
    queries = queries.reshape(ROWS, HEADS, NOPE + ROPE)
    query_rope = rotary(queries[:, :, NOPE:].astype(jnp.float32), lengths).astype(jnp.bfloat16)
    query_latent = jnp.einsum('rhn,hln->rhl', queries[:, :, :NOPE].astype(jnp.float32), w_key_up.astype(jnp.float32)).astype(jnp.bfloat16)
    latent_new = rms_norm(jnp.dot(normed, w_latent, preferred_element_type=jnp.float32), latent_gain).astype(jnp.bfloat16)
    key_raw = lax.dot_general(normed, w_rope_key, (((1,), (1,)), ((), ())), preferred_element_type=jnp.float32)
    key_new = rotary(key_raw, lengths).astype(jnp.bfloat16)
    score_scale = (NOPE + ROPE) ** (-0.5)
    block_count = ROWS // ROW_DEV

    def one_block(pieces):
        q_lat, q_rot, lat_new, k_new, lat_cache, rot_cache, lens = pieces
        mixed_latent = attend(q_lat, q_rot, lat_new, k_new, lat_cache, rot_cache, lens, score_scale)
        head_out = jnp.einsum('rhl,hlv->rhv', mixed_latent.astype(jnp.float32), w_value_up.astype(jnp.float32))
        return head_out.astype(jnp.bfloat16).reshape(ROW_DEV, HEADS * VHEAD)
    head_out = lax.map(one_block, (query_latent.reshape(block_count, ROW_DEV, HEADS, LATENT), query_rope.reshape(block_count, ROW_DEV, HEADS, ROPE), latent_new.reshape(block_count, ROW_DEV, LATENT), key_new.reshape(block_count, ROW_DEV, ROPE), latent_cache.reshape(block_count, ROW_DEV, LEN, LATENT), rope_cache.reshape(block_count, ROW_DEV, ROPE, LEN), lengths.reshape(block_count, ROW_DEV))).reshape(ROWS, HEADS * VHEAD)
    attention = jnp.dot(head_out, w_out, preferred_element_type=jnp.float32)
    middle = (hidden.astype(jnp.float32) + attention).astype(jnp.bfloat16)
    expert_in = rms_norm(middle.astype(jnp.float32), ffn_gain).astype(jnp.bfloat16)
    target, capacity = slot_targets(expert_ids, ROW_Q)
    row_ids = jnp.repeat(jnp.arange(ROWS, dtype=jnp.int32), TOPK)
    row_of = jnp.full((EXPERTS * capacity,), ROWS, jnp.int32).at[target.reshape(-1)].set(row_ids)
    padded = jnp.concatenate([expert_in, jnp.zeros((1, D), jnp.bfloat16)], axis=0)

    def one_expert(pieces):
        picked, gate_up, down_part = pieces
        rows_in = padded[picked]
        gate_part = jnp.dot(rows_in, gate_up[0].T, preferred_element_type=jnp.float32)
        up_part = jnp.dot(rows_in, gate_up[1].T, preferred_element_type=jnp.float32)
        activated = (jax.nn.silu(gate_part) * up_part).astype(jnp.bfloat16)
        return jnp.dot(activated, down_part, preferred_element_type=jnp.float32).astype(jnp.bfloat16)
    outputs = lax.map(one_expert, (row_of.reshape(EXPERTS, capacity), w_gate_up, w_down)).reshape(EXPERTS * capacity, D)
    routed = outputs[target.reshape(-1)].reshape(ROWS, TOPK, D).astype(jnp.float32)
    layer_out = middle.astype(jnp.float32) + lax.optimization_barrier(jnp.sum(route_weights[:, :, None] * routed, axis=1))
    return layer_out.astype(jnp.bfloat16)
```

```python
import jax
import jax.numpy as jnp
from jax import lax
from jax.sharding import PartitionSpec as P

EXPERTS = 64
MOST = 2
ROW_Q = 8


epsilon = 1e-06
far_below = -1e30


def rms_norm(values, norm_gain):
    mean_square = jnp.mean(values * values, axis=-1, keepdims=True)
    return values * lax.rsqrt(mean_square + epsilon) * norm_gain


def rotary(values, positions):
    half_width = values.shape[-1] // 2
    step_index = jnp.arange(half_width, dtype=jnp.float32)
    frequency = jnp.exp(-jnp.log(10000.0) * step_index / half_width)
    angles = positions.astype(jnp.float32)[:, None] * frequency[None, :]
    if values.ndim == 3:
        angles = angles[:, None, :]
    cosine = jnp.cos(angles)
    sine_part = jnp.sin(angles)
    first_half = values[..., :half_width]
    second = values[..., half_width:]
    return jnp.concatenate(
        [first_half * cosine - second * sine_part, second * cosine + first_half * sine_part],
        axis=-1,
    )


def slot_targets(expert_ids, block_rows):
    row_count, top_count = expert_ids.shape
    blocks = row_count // block_rows
    ids = expert_ids.reshape(blocks, block_rows, top_count)
    same = ids[:, :, :, None, None] == ids[:, None, None, :, :]
    row_index = jnp.arange(block_rows, dtype=jnp.int32)
    earlier = row_index[:, None, None, None] > row_index[None, None, :, None]
    rank_in = jnp.sum((same & earlier[None]).astype(jnp.int32), axis=(3, 4))
    capacity = blocks * MOST
    block_index = jnp.arange(blocks, dtype=jnp.int32)[:, None, None]
    target = ids * capacity + block_index * MOST + rank_in
    return (target.reshape(row_count, top_count), capacity)


def pack_rows(source, target, capacity):
    slot_count = EXPERTS * capacity
    hit_table = (
        target[:, :, None] == jnp.arange(slot_count, dtype=jnp.int32)[None, None, :]
    ).astype(jnp.bfloat16)
    hit_table = jnp.sum(hit_table, axis=1)
    packed = lax.dot_general(
        hit_table, source, (((0,), (0,)), ((), ())), preferred_element_type=jnp.float32
    )
    return packed.astype(jnp.bfloat16)


def expert_part(slot_rows, w_gate_up, w_down):
    gate_up = jnp.einsum(
        "secx,egfx->secgf", slot_rows, w_gate_up, preferred_element_type=jnp.float32
    )
    activated = (jax.nn.silu(gate_up[:, :, :, 0, :]) * gate_up[:, :, :, 1, :]).astype(jnp.bfloat16)
    return jnp.einsum("secf,efx->secx", activated, w_down, preferred_element_type=jnp.float32)


def section_sum(partial):
    sections = lax.axis_size("section")
    shifted = [
        lax.ppermute(partial, "section", [(i, (i + step) % sections) for i in range(sections)])
        for step in range(1, sections)
    ]
    held = [value.astype(jnp.float32) for value in [partial] + shifted]
    half = sections // 2
    pairs = [held[i] + held[i + half] for i in range(half)]
    return sum(pairs[1:], pairs[0])


def combine_rows(returned, target, route_weights):
    flat_out = returned.reshape(-1, returned.shape[-1])
    slots = jnp.arange(flat_out.shape[0], dtype=jnp.int32)
    hits = target[:, :, None] == slots[None, None, :]
    table = jnp.sum(jnp.where(hits, route_weights[:, :, None], 0.0), axis=1)
    upper = lax.reduce_precision(table, 8, 7)
    both = jnp.concatenate([upper, table - upper], axis=0).astype(jnp.bfloat16)
    sums = jnp.dot(both, flat_out, preferred_element_type=jnp.float32)
    return sums[: target.shape[0]] + sums[target.shape[0] :]


def attend(
    query_latent, query_rope, latent_new, key_new, latent_cache, rope_cache, lengths, score_scale
):
    scores = jnp.einsum(
        "rhl,rtl->rht", query_latent, latent_cache, preferred_element_type=jnp.float32
    )
    scores = scores + jnp.einsum(
        "rhp,rpt->rht", query_rope, rope_cache, preferred_element_type=jnp.float32
    )
    scores = scores * score_scale
    self_score = jnp.einsum(
        "rhl,rl->rh", query_latent, latent_new, preferred_element_type=jnp.float32
    )
    self_score = (
        self_score
        + jnp.einsum("rhp,rp->rh", query_rope, key_new, preferred_element_type=jnp.float32)
    ) * score_scale
    places = jnp.arange(latent_cache.shape[1], dtype=jnp.int32)
    valid_mask = places[None, None, :] < lengths[:, None, None]
    masked = jnp.where(valid_mask, scores, far_below)
    peak_score = jnp.maximum(jnp.max(masked, axis=2), self_score)
    weights = jnp.where(valid_mask, jnp.exp(masked - peak_score[:, :, None]), 0.0)
    self_weight = jnp.exp(self_score - peak_score)
    totals = jnp.sum(weights, axis=2) + self_weight
    prob_cache = (weights / totals[:, :, None]).astype(jnp.bfloat16)
    prob_self = (self_weight / totals).astype(jnp.bfloat16)
    mixed = jnp.einsum("rht,rtl->rhl", prob_cache, latent_cache, preferred_element_type=jnp.float32)
    mixed = (
        mixed
        + prob_self.astype(jnp.float32)[:, :, None] * latent_new.astype(jnp.float32)[:, None, :]
    )
    return mixed.astype(jnp.bfloat16)


def per_device(
    hidden,
    lengths,
    attn_gain,
    w_query,
    w_latent,
    latent_gain,
    w_rope_key,
    w_key_up,
    w_value_up,
    w_out,
    latent_cache,
    rope_cache,
    ffn_gain,
    expert_ids,
    route_weights,
    w_gate_up,
    w_down,
):
    devices = lax.axis_size("dev")
    row_count = hidden.shape[0]
    block_rows = ROW_Q
    model_width = hidden.shape[1]
    head_local = w_key_up.shape[0]
    nope_width = w_key_up.shape[2]
    rope_width = w_rope_key.shape[0]
    score_scale = (nope_width + rope_width) ** (-0.5)
    normed = rms_norm(hidden.astype(jnp.float32), attn_gain).astype(jnp.bfloat16)
    queries = jnp.dot(normed, w_query, preferred_element_type=jnp.float32).astype(jnp.bfloat16)
    queries = queries.reshape(row_count, head_local, nope_width + rope_width)
    query_rope = rotary(queries[:, :, nope_width:].astype(jnp.float32), lengths).astype(
        jnp.bfloat16
    )
    query_latent = jnp.einsum(
        "rhn,hln->rhl", queries[:, :, :nope_width], w_key_up, preferred_element_type=jnp.float32
    ).astype(jnp.bfloat16)
    latent_new = rms_norm(
        jnp.dot(normed, w_latent, preferred_element_type=jnp.float32), latent_gain
    ).astype(jnp.bfloat16)
    key_raw = lax.dot_general(
        normed, w_rope_key, (((1,), (1,)), ((), ())), preferred_element_type=jnp.float32
    )
    key_new = rotary(key_raw, lengths).astype(jnp.bfloat16)
    mixed_latent = attend(
        query_latent,
        query_rope,
        latent_new,
        key_new,
        latent_cache,
        rope_cache,
        lengths,
        score_scale,
    )
    head_out = jnp.einsum(
        "rhl,hlv->rhv", mixed_latent, w_value_up, preferred_element_type=jnp.float32
    ).astype(jnp.bfloat16)
    heads_flat = head_out.reshape(row_count, -1)
    partial_value = jnp.dot(heads_flat, w_out, preferred_element_type=jnp.float32)
    attention = section_sum(partial_value.astype(jnp.bfloat16))
    middle = (hidden.astype(jnp.float32) + attention).astype(jnp.bfloat16)
    expert_in = rms_norm(middle.astype(jnp.float32), ffn_gain).astype(jnp.bfloat16)
    target, capacity = slot_targets(expert_ids, block_rows)
    packed = pack_rows(expert_in, target, capacity).reshape(devices, -1, capacity, model_width)
    partial_out = expert_part(
        lax.all_to_all(packed, "dev", split_axis=0, concat_axis=0, tiled=True), w_gate_up, w_down
    )
    returned = lax.all_to_all(
        partial_out.astype(jnp.bfloat16), "dev", split_axis=0, concat_axis=0, tiled=True
    )
    routed = section_sum(combine_rows(returned, target, route_weights).astype(jnp.bfloat16))
    return (middle.astype(jnp.float32) + routed).astype(jnp.bfloat16)


def solution(mesh):
    in_specs = (
        P("dev", None),
        P("dev"),
        P(),
        P(None, "section"),
        P(),
        P(),
        P(),
        P("section", None, None),
        P("section", None, None),
        P("section", None),
        P("dev", None, None),
        P("dev", None, None),
        P(),
        P("dev", None),
        P("dev", None),
        P("dev", None, "section", None),
        P("dev", "section", None),
    )
    out_specs = P("dev", None)
    return jax.shard_map(
        per_device, mesh=mesh, in_specs=in_specs, out_specs=out_specs, check_vma=False
    )
```

```python
import jax
import jax.numpy as jnp
from jax import lax
from jax.experimental import pallas as pl
from jax.experimental.pallas import tpu as pltpu
from jax.sharding import PartitionSpec as P

EXPERTS = 64
MOST = 2
ROW_Q = 8
GROUP = 4


epsilon = 1e-06
far_below = -1e30


def rms_norm(values, norm_gain):
    mean_square = jnp.mean(values * values, axis=-1, keepdims=True)
    return values * lax.rsqrt(mean_square + epsilon) * norm_gain


def pack_rows(source, table):
    packed = lax.dot_general(
        table, source, (((0,), (0,)), ((), ())), preferred_element_type=jnp.float32
    )
    return packed.astype(jnp.bfloat16)


def expert_part(slot_rows, w_gate_up, w_down):
    gate_up = jnp.einsum(
        "secx,egfx->secgf", slot_rows, w_gate_up, preferred_element_type=jnp.float32
    )
    activated = (jax.nn.silu(gate_up[:, :, :, 0, :]) * gate_up[:, :, :, 1, :]).astype(jnp.bfloat16)
    return jnp.einsum("secf,efx->secx", activated, w_down, preferred_element_type=jnp.float32)


def section_sum(partial):
    sections = lax.axis_size("section")
    shifted = [
        lax.ppermute(partial, "section", [(i, (i + step) % sections) for i in range(sections)])
        for step in range(1, sections)
    ]
    held = [value.astype(jnp.float32) for value in [partial] + shifted]
    half = sections // 2
    pairs = [held[i] + held[i + half] for i in range(half)]
    return sum(pairs[1:], pairs[0])


def combine_rows(returned, mix):
    flat_out = returned.reshape(-1, returned.shape[-1])
    sums = jnp.dot(mix, flat_out, preferred_element_type=jnp.float32)
    half = mix.shape[0] // 2
    return sums[:half] + sums[half:]


def attend_kernel(
    hidden_ref, lengths_ref, attn_gain_ref, latent_gain_ref, ids_ref, weights_ref,
    w_query_hbm, w_latent_hbm, w_rope_hbm, w_key_up_hbm, latent_hbm, rope_hbm, w_value_up_hbm, w_out_hbm,
    partial_ref, table_ref, mix_ref,
    w_query, w_latent, w_rope, w_key_up, latent, rope, w_value_up, w_out,
    query_rows, turned_rows, mixed_rows, weight_sems, cache_sems,
):
    rows = hidden_ref.shape[0]
    heads, latent_width, nope_width = w_key_up.shape
    rope_width = w_rope.shape[0]
    slots = latent.shape[1]
    half = rope_width // 2
    head_width = nope_width + rope_width
    flat = rows * heads
    score_scale = head_width ** (-0.5)
    step_rows = GROUP
    steps = rows // step_rows
    tile = step_rows * heads

    early = [
        pltpu.make_async_copy(source, target, weight_sems.at[i])
        for i, (source, target) in enumerate(
            [
                (w_query_hbm, w_query),
                (w_key_up_hbm, w_key_up),
                (w_latent_hbm, w_latent),
                (w_rope_hbm, w_rope),
            ]
        )
    ]
    late = [
        pltpu.make_async_copy(source, target, weight_sems.at[len(early) + i])
        for i, (source, target) in enumerate([(w_value_up_hbm, w_value_up), (w_out_hbm, w_out)])
    ]
    cache = []
    for i in range(steps):
        span = pl.ds(i * step_rows, step_rows)
        cache.append(
            (
                pltpu.make_async_copy(latent_hbm.at[span], latent.at[span], cache_sems.at[i, 0]),
                pltpu.make_async_copy(rope_hbm.at[span], rope.at[span], cache_sems.at[i, 1]),
            )
        )
    for copy in early:
        copy.start()
    for pair in cache:
        for copy in pair:
            copy.start()
    for copy in late:
        copy.start()

    def count(shape, axis):
        return lax.broadcasted_iota(jnp.int32, shape, axis)

    slot_count = table_ref.shape[1]
    capacity = slot_count // EXPERTS
    slot_index = count((rows, slot_count), 1)
    slot_expert = slot_index // capacity
    slot_place = slot_index % capacity
    named = jnp.zeros((rows, slot_count), jnp.float32)
    weight = jnp.zeros((rows, slot_count), jnp.float32)
    for k in range(ids_ref.shape[1]):
        hit = ids_ref[:, k : k + 1] == slot_expert
        named = jnp.where(hit, 1.0, named)
        weight = jnp.where(hit, weights_ref[:, k : k + 1], weight)
    one, two = count((rows, rows), 0), count((rows, rows), 1)
    before = jnp.where((two < one) & (two // ROW_Q == one // ROW_Q), 1.0, 0.0)
    rank_in = jnp.dot(
        before.astype(jnp.bfloat16), named.astype(jnp.bfloat16), preferred_element_type=jnp.float32
    )
    wanted = (count((rows, slot_count), 0) // ROW_Q) * MOST + rank_in.astype(jnp.int32)
    taken = (slot_place == wanted) & (named > 0.0)
    table_ref[...] = jnp.where(taken, 1.0, 0.0).astype(jnp.bfloat16)
    weight = jnp.where(taken, weight, 0.0)
    upper = weight.astype(jnp.bfloat16)
    mix_ref[0:rows, :] = upper
    mix_ref[rows : 2 * rows, :] = (weight - upper.astype(jnp.float32)).astype(jnp.bfloat16)

    lengths = lengths_ref[...].astype(jnp.float32)
    repeat = jnp.where(count((flat, rows), 0) // heads == count((flat, rows), 1), 1.0, 0.0)
    flat_length = jnp.sum(repeat * lengths, axis=1, keepdims=True)
    same = jnp.where(one == two, 1.0, 0.0)
    row_length = jnp.sum(same * lengths, axis=1, keepdims=True)
    repeat = repeat.astype(jnp.bfloat16)
    place, other = count((flat, flat), 0), count((flat, flat), 1)
    order = jnp.where(place == (other % rows) * heads + other // rows, 1.0, 0.0).astype(jnp.bfloat16)
    back = jnp.where(other == (place % rows) * heads + place // rows, 1.0, 0.0).astype(jnp.bfloat16)
    frequency = jnp.exp(
        -jnp.log(10000.0) * count((1, half), 1).astype(jnp.float32) / half
    )
    angles = row_length * frequency
    cosine, sine_part = jnp.cos(angles), jnp.sin(angles)

    def turned(first_half, second):
        return jnp.concatenate(
            [first_half * cosine - second * sine_part, second * cosine + first_half * sine_part],
            axis=1,
        ).astype(jnp.bfloat16)

    values = hidden_ref[...].astype(jnp.float32)
    mean_square = jnp.mean(values * values, axis=1, keepdims=True)
    normed = (values * lax.rsqrt(mean_square + epsilon) * attn_gain_ref[...]).astype(jnp.bfloat16)

    early[0].wait()
    queries = jnp.dot(normed, w_query[...], preferred_element_type=jnp.float32).astype(jnp.bfloat16)
    early[1].wait()
    by_head, turned_by_head = [], []
    for h in range(heads):
        start = h * head_width
        nope = queries[:, start : start + nope_width]
        by_head.append(
            lax.dot_general(
                nope, w_key_up[h], (((1,), (1,)), ((), ())), preferred_element_type=jnp.float32
            ).astype(jnp.bfloat16)
        )
        middle = start + nope_width
        turned_by_head.append(
            turned(
                queries[:, middle : middle + half].astype(jnp.float32),
                queries[:, middle + half : middle + rope_width].astype(jnp.float32),
            )
        )
    query_rows[...] = jnp.dot(
        order, jnp.concatenate(by_head, axis=0), preferred_element_type=jnp.float32
    ).astype(jnp.bfloat16)
    turned_rows[...] = jnp.dot(
        order, jnp.concatenate(turned_by_head, axis=0), preferred_element_type=jnp.float32
    ).astype(jnp.bfloat16)

    early[2].wait()
    latent_raw = jnp.dot(normed, w_latent[...], preferred_element_type=jnp.float32)
    mean_square = jnp.mean(latent_raw * latent_raw, axis=1, keepdims=True)
    latent_new = (latent_raw * lax.rsqrt(mean_square + epsilon) * latent_gain_ref[...]).astype(
        jnp.bfloat16
    )
    early[3].wait()
    key_raw = lax.dot_general(
        normed, w_rope[...], (((1,), (1,)), ((), ())), preferred_element_type=jnp.float32
    )
    key_new = turned(key_raw[:, :half], key_raw[:, half:])
    latent_flat = jnp.dot(repeat, latent_new, preferred_element_type=jnp.float32)
    key_flat = jnp.dot(repeat, key_new, preferred_element_type=jnp.float32)
    self_score = (
        jnp.sum(query_rows[...].astype(jnp.float32) * latent_flat, axis=1, keepdims=True)
        + jnp.sum(turned_rows[...].astype(jnp.float32) * key_flat, axis=1, keepdims=True)
    ) * score_scale

    owner = count((tile, 1), 0) // heads
    places = count((tile, slots), 1).astype(jnp.float32)

    def scores_of(i):
        span = slice(i * tile, (i + 1) * tile)
        query, query_turned = query_rows[span, :], turned_rows[span, :]
        total = jnp.zeros((tile, slots), jnp.float32)
        for j in range(step_rows):
            row = i * step_rows + j
            part = lax.dot_general(
                query, latent[row], (((1,), (1,)), ((), ())), preferred_element_type=jnp.float32
            ) + jnp.dot(query_turned, rope[row], preferred_element_type=jnp.float32)
            total = jnp.where(owner == j, part, total)
        return total * score_scale

    def mix(i, scores):
        span = slice(i * tile, (i + 1) * tile)
        valid = places < flat_length[span]
        own = self_score[span]
        masked = jnp.where(valid, scores, far_below)
        peak = jnp.maximum(jnp.max(masked, axis=1, keepdims=True), own)
        weights = jnp.where(valid, jnp.exp(masked - peak), 0.0)
        self_weight = jnp.exp(own - peak)
        total = jnp.sum(weights, axis=1, keepdims=True) + self_weight
        probs = (weights / total).astype(jnp.bfloat16)
        prob_self = (self_weight / total).astype(jnp.bfloat16).astype(jnp.float32)
        mixed = jnp.zeros((tile, latent_width), jnp.float32)
        for j in range(step_rows):
            part = jnp.dot(probs, latent[i * step_rows + j], preferred_element_type=jnp.float32)
            mixed = jnp.where(owner == j, part, mixed)
        mixed_rows[span, :] = (mixed + prob_self * latent_flat[span]).astype(jnp.bfloat16)

    held = None
    for i in range(steps):
        for copy in cache[i]:
            copy.wait()
        scores = scores_of(i)
        if held is not None:
            mix(i - 1, held)
        held = scores
    mix(steps - 1, held)

    for copy in late:
        copy.wait()
    by_row = jnp.dot(back, mixed_rows[...], preferred_element_type=jnp.float32).astype(jnp.bfloat16)
    outs = [
        jnp.dot(
            by_row[h * rows : (h + 1) * rows], w_value_up[h], preferred_element_type=jnp.float32
        ).astype(jnp.bfloat16)
        for h in range(heads)
    ]
    partial_ref[...] = jnp.dot(
        jnp.concatenate(outs, axis=1), w_out[...], preferred_element_type=jnp.float32
    ).astype(jnp.bfloat16)


def attend_rows(
    hidden, lengths, attn_gain, latent_gain, expert_ids, route_weights,
    w_query, w_latent, w_rope_key, w_key_up, latent_cache, rope_cache, w_value_up, w_out,
):
    rows, model_width = hidden.shape
    heads, latent_width = w_key_up.shape[:2]
    capacity = rows // ROW_Q * MOST
    slot_count = EXPERTS * capacity
    big = (w_query, w_latent, w_rope_key, w_key_up, latent_cache, rope_cache, w_value_up, w_out)
    steps = rows // GROUP
    return pl.pallas_call(
        attend_kernel,
        out_shape=(
            jax.ShapeDtypeStruct((rows, model_width), jnp.bfloat16),
            jax.ShapeDtypeStruct((rows, slot_count), jnp.bfloat16),
            jax.ShapeDtypeStruct((2 * rows, slot_count), jnp.bfloat16),
        ),
        in_specs=[pl.BlockSpec(memory_space=pltpu.VMEM)] * 6
        + [pl.BlockSpec(memory_space=pl.ANY)] * len(big),
        out_specs=(pl.BlockSpec(memory_space=pltpu.VMEM),) * 3,
        scratch_shapes=[pltpu.VMEM(array.shape, array.dtype) for array in big]
        + [
            pltpu.VMEM((rows * heads, latent_width), jnp.bfloat16),
            pltpu.VMEM((rows * heads, w_rope_key.shape[0]), jnp.bfloat16),
            pltpu.VMEM((rows * heads, latent_width), jnp.bfloat16),
            pltpu.SemaphoreType.DMA((6,)),
            pltpu.SemaphoreType.DMA((steps, 2)),
        ],
        compiler_params=pltpu.CompilerParams(vmem_limit_bytes=40 << 20),
        name="attend_rows",
    )(
        hidden, lengths.reshape(1, rows), attn_gain.reshape(1, -1), latent_gain.reshape(1, -1),
        expert_ids, route_weights, *big,
    )


def per_device(
    hidden,
    lengths,
    attn_gain,
    w_query,
    w_latent,
    latent_gain,
    w_rope_key,
    w_key_up,
    w_value_up,
    w_out,
    latent_cache,
    rope_cache,
    ffn_gain,
    expert_ids,
    route_weights,
    w_gate_up,
    w_down,
):
    devices = lax.axis_size("dev")
    model_width = hidden.shape[1]
    partial_value, table, mix = attend_rows(
        hidden, lengths, attn_gain, latent_gain, expert_ids, route_weights,
        w_query, w_latent, w_rope_key, w_key_up, latent_cache, rope_cache, w_value_up, w_out,
    )
    middle = (hidden.astype(jnp.float32) + section_sum(partial_value)).astype(jnp.bfloat16)
    expert_in = rms_norm(middle.astype(jnp.float32), ffn_gain).astype(jnp.bfloat16)
    capacity = table.shape[1] // EXPERTS
    packed = pack_rows(expert_in, table).reshape(devices, -1, capacity, model_width)
    partial_out = expert_part(
        lax.all_to_all(packed, "dev", split_axis=0, concat_axis=0, tiled=True), w_gate_up, w_down
    )
    returned = lax.all_to_all(
        partial_out.astype(jnp.bfloat16), "dev", split_axis=0, concat_axis=0, tiled=True
    )
    routed = section_sum(combine_rows(returned, mix).astype(jnp.bfloat16))
    return (middle.astype(jnp.float32) + routed).astype(jnp.bfloat16)


def solution(mesh):
    in_specs = (
        P("dev", None),
        P("dev"),
        P(),
        P(None, "section"),
        P(),
        P(),
        P(),
        P("section", None, None),
        P("section", None, None),
        P("section", None),
        P("dev", None, None),
        P("dev", None, None),
        P(),
        P("dev", None),
        P("dev", None),
        P("dev", None, "section", None),
        P("dev", "section", None),
    )
    out_specs = P("dev", None)
    return jax.shard_map(
        per_device, mesh=mesh, in_specs=in_specs, out_specs=out_specs, check_vma=False
    )
```

```python
import jax
import jax.numpy as jnp
from jax import lax
from jax.experimental import pallas as pl
from jax.experimental.pallas import tpu as pltpu
from jax.sharding import PartitionSpec as P

EXPERTS = 64
MOST = 2
ROW_Q = 8
GROUP = 4


epsilon = 1e-06
far_below = -1e30


def rms_norm(values, norm_gain):
    mean_square = jnp.mean(values * values, axis=-1, keepdims=True)
    return values * lax.rsqrt(mean_square + epsilon) * norm_gain


def pack_rows(source, table):
    packed = lax.dot_general(
        table, source, (((0,), (0,)), ((), ())), preferred_element_type=jnp.float32
    )
    return packed.astype(jnp.bfloat16)


def expert_part(slot_rows, w_gate_up, w_down):
    gate_up = jnp.einsum(
        "secx,egfx->secgf", slot_rows, w_gate_up, preferred_element_type=jnp.float32
    )
    activated = (jax.nn.silu(gate_up[:, :, :, 0, :]) * gate_up[:, :, :, 1, :]).astype(jnp.bfloat16)
    return jnp.einsum("secf,efx->secx", activated, w_down, preferred_element_type=jnp.float32)


def section_sum(partial):
    sections = lax.axis_size("section")
    shifted = [
        lax.ppermute(partial, "section", [(i, (i + step) % sections) for i in range(sections)])
        for step in range(1, sections)
    ]
    held = [value.astype(jnp.float32) for value in [partial] + shifted]
    half = sections // 2
    pairs = [held[i] + held[i + half] for i in range(half)]
    return sum(pairs[1:], pairs[0])


def combine_rows(returned, mix):
    flat_out = returned.reshape(-1, returned.shape[-1])
    sums = jnp.dot(mix, flat_out, preferred_element_type=jnp.float32)
    half = mix.shape[0] // 2
    return sums[:half] + sums[half:]


def attend_kernel(*refs):
    sources, rest = refs[:14], refs[14:]
    partial_ref, table_ref, mix_ref = rest[:3]
    held_refs, rest = rest[3:17], rest[17:]
    query_rows, turned_rows, mixed_rows, load_sems, cache_sems = rest
    (
        hidden_ref, lengths_ref, attn_gain_ref, latent_gain_ref, ids_ref, weights_ref,
        w_query, w_key_up, w_latent, w_rope, w_value_up, w_out, latent, rope,
    ) = held_refs
    latent_hbm, rope_hbm = sources[12:]
    rows = hidden_ref.shape[0]
    heads, latent_width, nope_width = w_key_up.shape
    rope_width = w_rope.shape[0]
    slots = latent.shape[1]
    half = rope_width // 2
    head_width = nope_width + rope_width
    flat = rows * heads
    score_scale = head_width ** (-0.5)
    step_rows = GROUP
    steps = rows // step_rows
    tile = step_rows * heads

    loads = [
        pltpu.make_async_copy(source, target, load_sems.at[i])
        for i, (source, target) in enumerate(zip(sources[:12], held_refs[:12]))
    ]
    small, early, late = loads[:6], loads[6:10], loads[10:]
    cache = []
    for i in range(steps):
        span = pl.ds(i * step_rows, step_rows)
        cache.append(
            (
                pltpu.make_async_copy(latent_hbm.at[span], latent.at[span], cache_sems.at[i, 0]),
                pltpu.make_async_copy(rope_hbm.at[span], rope.at[span], cache_sems.at[i, 1]),
            )
        )
    for copy in small + early:
        copy.start()
    for pair in cache:
        for copy in pair:
            copy.start()
    for copy in late:
        copy.start()

    def count(shape, axis):
        return lax.broadcasted_iota(jnp.int32, shape, axis)

    one, two = count((rows, rows), 0), count((rows, rows), 1)
    same = jnp.where(one == two, 1.0, 0.0)

    def column(row):
        return jnp.sum(same * row.astype(jnp.float32), axis=1, keepdims=True)

    for copy in small:
        copy.wait()
    slot_count = table_ref.shape[1]
    capacity = slot_count // EXPERTS
    slot_index = count((rows, slot_count), 1)
    slot_expert = slot_index // capacity
    slot_place = slot_index % capacity
    named = jnp.zeros((rows, slot_count), jnp.float32)
    weight = jnp.zeros((rows, slot_count), jnp.float32)
    for k in range(ids_ref.shape[0]):
        hit = column(ids_ref[k : k + 1, :]).astype(jnp.int32) == slot_expert
        named = jnp.where(hit, 1.0, named)
        weight = jnp.where(hit, column(weights_ref[k : k + 1, :]), weight)
    before = jnp.where((two < one) & (two // ROW_Q == one // ROW_Q), 1.0, 0.0)
    rank_in = jnp.dot(
        before.astype(jnp.bfloat16), named.astype(jnp.bfloat16), preferred_element_type=jnp.float32
    )
    wanted = (count((rows, slot_count), 0) // ROW_Q) * MOST + rank_in.astype(jnp.int32)
    taken = (slot_place == wanted) & (named > 0.0)
    table_ref[...] = jnp.where(taken, 1.0, 0.0).astype(jnp.bfloat16)
    weight = jnp.where(taken, weight, 0.0)
    upper = weight.astype(jnp.bfloat16)
    mix_ref[0:rows, :] = upper
    mix_ref[rows : 2 * rows, :] = (weight - upper.astype(jnp.float32)).astype(jnp.bfloat16)

    lengths = lengths_ref[...].astype(jnp.float32)
    repeat = jnp.where(count((flat, rows), 0) // heads == count((flat, rows), 1), 1.0, 0.0)
    flat_length = jnp.sum(repeat * lengths, axis=1, keepdims=True)
    row_length = column(lengths)
    repeat = repeat.astype(jnp.bfloat16)
    place, other = count((flat, flat), 0), count((flat, flat), 1)
    order = jnp.where(place == (other % rows) * heads + other // rows, 1.0, 0.0).astype(jnp.bfloat16)
    back = jnp.where(other == (place % rows) * heads + place // rows, 1.0, 0.0).astype(jnp.bfloat16)
    frequency = jnp.exp(
        -jnp.log(10000.0) * count((1, half), 1).astype(jnp.float32) / half
    )
    angles = row_length * frequency
    cosine, sine_part = jnp.cos(angles), jnp.sin(angles)

    def turned(first_half, second):
        return jnp.concatenate(
            [first_half * cosine - second * sine_part, second * cosine + first_half * sine_part],
            axis=1,
        ).astype(jnp.bfloat16)

    values = hidden_ref[...].astype(jnp.float32)
    mean_square = jnp.mean(values * values, axis=1, keepdims=True)
    normed = (values * lax.rsqrt(mean_square + epsilon) * attn_gain_ref[...]).astype(jnp.bfloat16)

    early[0].wait()
    queries = jnp.dot(normed, w_query[...], preferred_element_type=jnp.float32).astype(jnp.bfloat16)
    early[1].wait()
    by_head, turned_by_head = [], []
    for h in range(heads):
        start = h * head_width
        nope = queries[:, start : start + nope_width]
        by_head.append(
            lax.dot_general(
                nope, w_key_up[h], (((1,), (1,)), ((), ())), preferred_element_type=jnp.float32
            ).astype(jnp.bfloat16)
        )
        middle = start + nope_width
        turned_by_head.append(
            turned(
                queries[:, middle : middle + half].astype(jnp.float32),
                queries[:, middle + half : middle + rope_width].astype(jnp.float32),
            )
        )
    query_rows[...] = jnp.dot(
        order, jnp.concatenate(by_head, axis=0), preferred_element_type=jnp.float32
    ).astype(jnp.bfloat16)
    turned_rows[...] = jnp.dot(
        order, jnp.concatenate(turned_by_head, axis=0), preferred_element_type=jnp.float32
    ).astype(jnp.bfloat16)

    early[2].wait()
    latent_raw = jnp.dot(normed, w_latent[...], preferred_element_type=jnp.float32)
    mean_square = jnp.mean(latent_raw * latent_raw, axis=1, keepdims=True)
    latent_new = (latent_raw * lax.rsqrt(mean_square + epsilon) * latent_gain_ref[...]).astype(
        jnp.bfloat16
    )
    early[3].wait()
    key_raw = lax.dot_general(
        normed, w_rope[...], (((1,), (1,)), ((), ())), preferred_element_type=jnp.float32
    )
    key_new = turned(key_raw[:, :half], key_raw[:, half:])
    latent_flat = jnp.dot(repeat, latent_new, preferred_element_type=jnp.float32)
    key_flat = jnp.dot(repeat, key_new, preferred_element_type=jnp.float32)
    self_score = (
        jnp.sum(query_rows[...].astype(jnp.float32) * latent_flat, axis=1, keepdims=True)
        + jnp.sum(turned_rows[...].astype(jnp.float32) * key_flat, axis=1, keepdims=True)
    ) * score_scale

    owner = count((tile, 1), 0) // heads
    places = count((tile, slots), 1).astype(jnp.float32)

    def scores_of(i):
        span = slice(i * tile, (i + 1) * tile)
        query, query_turned = query_rows[span, :], turned_rows[span, :]
        total = jnp.zeros((tile, slots), jnp.float32)
        for j in range(step_rows):
            row = i * step_rows + j
            part = lax.dot_general(
                query, latent[row], (((1,), (1,)), ((), ())), preferred_element_type=jnp.float32
            ) + jnp.dot(query_turned, rope[row], preferred_element_type=jnp.float32)
            total = jnp.where(owner == j, part, total)
        return total * score_scale

    def mix(i, scores):
        span = slice(i * tile, (i + 1) * tile)
        valid = places < flat_length[span]
        own = self_score[span]
        masked = jnp.where(valid, scores, far_below)
        peak = jnp.maximum(jnp.max(masked, axis=1, keepdims=True), own)
        weights = jnp.where(valid, jnp.exp(masked - peak), 0.0)
        self_weight = jnp.exp(own - peak)
        total = jnp.sum(weights, axis=1, keepdims=True) + self_weight
        probs = (weights / total).astype(jnp.bfloat16)
        prob_self = (self_weight / total).astype(jnp.bfloat16).astype(jnp.float32)
        mixed = jnp.zeros((tile, latent_width), jnp.float32)
        for j in range(step_rows):
            part = jnp.dot(probs, latent[i * step_rows + j], preferred_element_type=jnp.float32)
            mixed = jnp.where(owner == j, part, mixed)
        mixed_rows[span, :] = (mixed + prob_self * latent_flat[span]).astype(jnp.bfloat16)

    held = None
    for i in range(steps):
        for copy in cache[i]:
            copy.wait()
        scores = scores_of(i)
        if held is not None:
            mix(i - 1, held)
        held = scores
    mix(steps - 1, held)

    for copy in late:
        copy.wait()
    by_row = jnp.dot(back, mixed_rows[...], preferred_element_type=jnp.float32).astype(jnp.bfloat16)
    outs = [
        jnp.dot(
            by_row[h * rows : (h + 1) * rows], w_value_up[h], preferred_element_type=jnp.float32
        ).astype(jnp.bfloat16)
        for h in range(heads)
    ]
    partial_ref[...] = jnp.dot(
        jnp.concatenate(outs, axis=1), w_out[...], preferred_element_type=jnp.float32
    ).astype(jnp.bfloat16)


def attend_rows(
    hidden, lengths, attn_gain, latent_gain, expert_ids, route_weights,
    w_query, w_latent, w_rope_key, w_key_up, latent_cache, rope_cache, w_value_up, w_out,
):
    rows, model_width = hidden.shape
    heads, latent_width = w_key_up.shape[:2]
    capacity = rows // ROW_Q * MOST
    slot_count = EXPERTS * capacity
    sources = (
        hidden, lengths.reshape(1, rows), attn_gain.reshape(1, -1), latent_gain.reshape(1, -1),
        expert_ids.T, route_weights.T, w_query, w_key_up, w_latent, w_rope_key, w_value_up, w_out,
        latent_cache, rope_cache,
    )
    steps = rows // GROUP
    return pl.pallas_call(
        attend_kernel,
        out_shape=(
            jax.ShapeDtypeStruct((rows, model_width), jnp.bfloat16),
            jax.ShapeDtypeStruct((rows, slot_count), jnp.bfloat16),
            jax.ShapeDtypeStruct((2 * rows, slot_count), jnp.bfloat16),
        ),
        in_specs=[pl.BlockSpec(memory_space=pltpu.HBM)] * len(sources),
        out_specs=(pl.BlockSpec(memory_space=pltpu.VMEM),) * 3,
        scratch_shapes=[pltpu.VMEM(array.shape, array.dtype) for array in sources]
        + [
            pltpu.VMEM((rows * heads, latent_width), jnp.bfloat16),
            pltpu.VMEM((rows * heads, w_rope_key.shape[0]), jnp.bfloat16),
            pltpu.VMEM((rows * heads, latent_width), jnp.bfloat16),
            pltpu.SemaphoreType.DMA((12,)),
            pltpu.SemaphoreType.DMA((steps, 2)),
        ],
        compiler_params=pltpu.CompilerParams(vmem_limit_bytes=40 << 20),
        name="attend_rows",
    )(*[pltpu.with_memory_space_constraint(array, pltpu.HBM) for array in sources])


def per_device(
    hidden,
    lengths,
    attn_gain,
    w_query,
    w_latent,
    latent_gain,
    w_rope_key,
    w_key_up,
    w_value_up,
    w_out,
    latent_cache,
    rope_cache,
    ffn_gain,
    expert_ids,
    route_weights,
    w_gate_up,
    w_down,
):
    devices = lax.axis_size("dev")
    model_width = hidden.shape[1]
    partial_value, table, mix = attend_rows(
        hidden, lengths, attn_gain, latent_gain, expert_ids, route_weights,
        w_query, w_latent, w_rope_key, w_key_up, latent_cache, rope_cache, w_value_up, w_out,
    )
    middle = (hidden.astype(jnp.float32) + section_sum(partial_value)).astype(jnp.bfloat16)
    expert_in = rms_norm(middle.astype(jnp.float32), ffn_gain).astype(jnp.bfloat16)
    capacity = table.shape[1] // EXPERTS
    packed = pack_rows(expert_in, table).reshape(devices, -1, capacity, model_width)
    partial_out = expert_part(
        lax.all_to_all(packed, "dev", split_axis=0, concat_axis=0, tiled=True), w_gate_up, w_down
    )
    returned = lax.all_to_all(
        partial_out.astype(jnp.bfloat16), "dev", split_axis=0, concat_axis=0, tiled=True
    )
    routed = section_sum(combine_rows(returned, mix).astype(jnp.bfloat16))
    return (middle.astype(jnp.float32) + routed).astype(jnp.bfloat16)


def solution(mesh):
    in_specs = (
        P("dev", None),
        P("dev"),
        P(),
        P(None, "section"),
        P(),
        P(),
        P(),
        P("section", None, None),
        P("section", None, None),
        P("section", None),
        P("dev", None, None),
        P("dev", None, None),
        P(),
        P("dev", None),
        P("dev", None),
        P("dev", None, "section", None),
        P("dev", "section", None),
    )
    out_specs = P("dev", None)
    return jax.shard_map(
        per_device, mesh=mesh, in_specs=in_specs, out_specs=out_specs, check_vma=False
    )
```

```python
import jax
import jax.numpy as jnp
from jax import lax
from jax.experimental import pallas as pl
from jax.experimental.pallas import tpu as pltpu
from jax.sharding import PartitionSpec as P

EXPERTS = 64
MOST = 2
ROW_Q = 8
GROUPS = (16, 16)


epsilon = 1e-06
far_below = -1e30


def rms_norm(values, norm_gain):
    mean_square = jnp.mean(values * values, axis=-1, keepdims=True)
    return values * lax.rsqrt(mean_square + epsilon) * norm_gain


def pack_rows(source, table):
    packed = lax.dot_general(
        table, source, (((0,), (0,)), ((), ())), preferred_element_type=jnp.float32
    )
    return packed.astype(jnp.bfloat16)


def expert_part(slot_rows, w_gate_up, w_down):
    gate_up = jnp.einsum(
        "secx,egfx->secgf", slot_rows, w_gate_up, preferred_element_type=jnp.float32
    )
    activated = (jax.nn.silu(gate_up[:, :, :, 0, :]) * gate_up[:, :, :, 1, :]).astype(jnp.bfloat16)
    return jnp.einsum("secf,efx->secx", activated, w_down, preferred_element_type=jnp.float32)


def section_sum(partial):
    sections = lax.axis_size("section")
    shifted = [
        lax.ppermute(partial, "section", [(i, (i + step) % sections) for i in range(sections)])
        for step in range(1, sections)
    ]
    held = [value.astype(jnp.float32) for value in [partial] + shifted]
    half = sections // 2
    pairs = [held[i] + held[i + half] for i in range(half)]
    return sum(pairs[1:], pairs[0])


def combine_rows(returned, mix):
    flat_out = returned.reshape(-1, returned.shape[-1])
    sums = jnp.dot(mix, flat_out, preferred_element_type=jnp.float32)
    half = mix.shape[0] // 2
    return sums[:half] + sums[half:]


def attend_kernel(*refs):
    sources, rest = refs[:14], refs[14:]
    partial_ref, table_ref, mix_ref = rest[:3]
    held_refs, rest = rest[3:17], rest[17:]
    query_rows, turned_rows, mixed_rows, load_sems, cache_sems = rest
    (
        hidden_ref, lengths_ref, attn_gain_ref, latent_gain_ref, ids_ref, weights_ref,
        w_query, w_key_up, w_latent, w_rope, w_value_up, w_out, latent, rope,
    ) = held_refs
    latent_hbm, rope_hbm = sources[12:]
    rows = hidden_ref.shape[0]
    heads, latent_width, nope_width = w_key_up.shape
    rope_width = w_rope.shape[0]
    slots = latent.shape[1]
    half = rope_width // 2
    head_width = nope_width + rope_width
    flat = rows * heads
    score_scale = head_width ** (-0.5)
    starts = [sum(GROUPS[:i]) for i in range(len(GROUPS))]

    loads = [
        pltpu.make_async_copy(source, target, load_sems.at[i])
        for i, (source, target) in enumerate(zip(sources[:12], held_refs[:12]))
    ]
    small, early, late = loads[:6], loads[6:10], loads[10:]
    cache = []
    for i, (first, size) in enumerate(zip(starts, GROUPS)):
        span = pl.ds(first, size)
        cache.append(
            (
                pltpu.make_async_copy(latent_hbm.at[span], latent.at[span], cache_sems.at[i, 0]),
                pltpu.make_async_copy(rope_hbm.at[span], rope.at[span], cache_sems.at[i, 1]),
            )
        )
    for copy in small + early:
        copy.start()
    for pair in cache:
        for copy in pair:
            copy.start()
    for copy in late:
        copy.start()

    def count(shape, axis):
        return lax.broadcasted_iota(jnp.int32, shape, axis)

    one, two = count((rows, rows), 0), count((rows, rows), 1)
    same = jnp.where(one == two, 1.0, 0.0)

    def column(row):
        return jnp.sum(same * row.astype(jnp.float32), axis=1, keepdims=True)

    for copy in small:
        copy.wait()
    slot_count = table_ref.shape[1]
    capacity = slot_count // EXPERTS
    slot_index = count((rows, slot_count), 1)
    slot_expert = slot_index // capacity
    slot_place = slot_index % capacity
    named = jnp.zeros((rows, slot_count), jnp.float32)
    weight = jnp.zeros((rows, slot_count), jnp.float32)
    for k in range(ids_ref.shape[0]):
        hit = column(ids_ref[k : k + 1, :]).astype(jnp.int32) == slot_expert
        named = jnp.where(hit, 1.0, named)
        weight = jnp.where(hit, column(weights_ref[k : k + 1, :]), weight)
    before = jnp.where((two < one) & (two // ROW_Q == one // ROW_Q), 1.0, 0.0)
    rank_in = jnp.dot(
        before.astype(jnp.bfloat16), named.astype(jnp.bfloat16), preferred_element_type=jnp.float32
    )
    wanted = (count((rows, slot_count), 0) // ROW_Q) * MOST + rank_in.astype(jnp.int32)
    taken = (slot_place == wanted) & (named > 0.0)
    table_ref[...] = jnp.where(taken, 1.0, 0.0).astype(jnp.bfloat16)
    weight = jnp.where(taken, weight, 0.0)
    upper = weight.astype(jnp.bfloat16)
    mix_ref[0:rows, :] = upper
    mix_ref[rows : 2 * rows, :] = (weight - upper.astype(jnp.float32)).astype(jnp.bfloat16)

    lengths = lengths_ref[...].astype(jnp.float32)
    repeat = jnp.where(count((flat, rows), 0) // heads == count((flat, rows), 1), 1.0, 0.0)
    flat_length = jnp.sum(repeat * lengths, axis=1, keepdims=True)
    row_length = column(lengths)
    repeat = repeat.astype(jnp.bfloat16)
    place, other = count((flat, flat), 0), count((flat, flat), 1)
    order = jnp.where(place == (other % rows) * heads + other // rows, 1.0, 0.0).astype(jnp.bfloat16)
    back = jnp.where(other == (place % rows) * heads + place // rows, 1.0, 0.0).astype(jnp.bfloat16)
    frequency = jnp.exp(
        -jnp.log(10000.0) * count((1, half), 1).astype(jnp.float32) / half
    )
    angles = row_length * frequency
    cosine, sine_part = jnp.cos(angles), jnp.sin(angles)

    def turned(first_half, second):
        return jnp.concatenate(
            [first_half * cosine - second * sine_part, second * cosine + first_half * sine_part],
            axis=1,
        ).astype(jnp.bfloat16)

    values = hidden_ref[...].astype(jnp.float32)
    mean_square = jnp.mean(values * values, axis=1, keepdims=True)
    normed = (values * lax.rsqrt(mean_square + epsilon) * attn_gain_ref[...]).astype(jnp.bfloat16)

    early[0].wait()
    queries = jnp.dot(normed, w_query[...], preferred_element_type=jnp.float32).astype(jnp.bfloat16)
    early[1].wait()
    by_head, turned_by_head = [], []
    for h in range(heads):
        start = h * head_width
        nope = queries[:, start : start + nope_width]
        by_head.append(
            lax.dot_general(
                nope, w_key_up[h], (((1,), (1,)), ((), ())), preferred_element_type=jnp.float32
            ).astype(jnp.bfloat16)
        )
        middle = start + nope_width
        turned_by_head.append(
            turned(
                queries[:, middle : middle + half].astype(jnp.float32),
                queries[:, middle + half : middle + rope_width].astype(jnp.float32),
            )
        )
    query_rows[...] = jnp.dot(
        order, jnp.concatenate(by_head, axis=0), preferred_element_type=jnp.float32
    ).astype(jnp.bfloat16)
    turned_rows[...] = jnp.dot(
        order, jnp.concatenate(turned_by_head, axis=0), preferred_element_type=jnp.float32
    ).astype(jnp.bfloat16)

    early[2].wait()
    latent_raw = jnp.dot(normed, w_latent[...], preferred_element_type=jnp.float32)
    mean_square = jnp.mean(latent_raw * latent_raw, axis=1, keepdims=True)
    latent_new = (latent_raw * lax.rsqrt(mean_square + epsilon) * latent_gain_ref[...]).astype(
        jnp.bfloat16
    )
    early[3].wait()
    key_raw = lax.dot_general(
        normed, w_rope[...], (((1,), (1,)), ((), ())), preferred_element_type=jnp.float32
    )
    key_new = turned(key_raw[:, :half], key_raw[:, half:])
    latent_flat = jnp.dot(repeat, latent_new, preferred_element_type=jnp.float32)
    key_flat = jnp.dot(repeat, key_new, preferred_element_type=jnp.float32)
    self_score = (
        jnp.sum(query_rows[...].astype(jnp.float32) * latent_flat, axis=1, keepdims=True)
        + jnp.sum(turned_rows[...].astype(jnp.float32) * key_flat, axis=1, keepdims=True)
    ) * score_scale

    def scores_of(first, size):
        tile = size * heads
        span = slice(first * heads, first * heads + tile)
        query, query_turned = query_rows[span, :], turned_rows[span, :]
        owner = count((tile, 1), 0) // heads
        lane_owner = count((1, tile), 1) // heads
        total = jnp.zeros((tile, slots), jnp.float32)
        across = jnp.zeros((slots, tile), jnp.float32)
        for j in range(size):
            part = lax.dot_general(
                latent[first + j], query, (((1,), (1,)), ((), ())), preferred_element_type=jnp.float32
            )
            across = jnp.where(lane_owner == j, part, across)
            part = jnp.dot(query_turned, rope[first + j], preferred_element_type=jnp.float32)
            total = jnp.where(owner == j, part, total)
        return (across.T + total) * score_scale

    def mix(first, size, scores):
        tile = size * heads
        span = slice(first * heads, first * heads + tile)
        valid = count((tile, slots), 1).astype(jnp.float32) < flat_length[span]
        own = self_score[span]
        masked = jnp.where(valid, scores, far_below)
        peak = jnp.maximum(jnp.max(masked, axis=1, keepdims=True), own)
        weights = jnp.where(valid, jnp.exp(masked - peak), 0.0)
        self_weight = jnp.exp(own - peak)
        total = jnp.sum(weights, axis=1, keepdims=True) + self_weight
        probs = (weights / total).astype(jnp.bfloat16)
        prob_self = (self_weight / total).astype(jnp.bfloat16).astype(jnp.float32)
        owner = count((tile, 1), 0) // heads
        mixed = jnp.zeros((tile, latent_width), jnp.float32)
        for j in range(size):
            part = jnp.dot(probs, latent[first + j], preferred_element_type=jnp.float32)
            mixed = jnp.where(owner == j, part, mixed)
        mixed_rows[span, :] = (mixed + prob_self * latent_flat[span]).astype(jnp.bfloat16)

    held = None
    for i, group in enumerate(zip(starts, GROUPS)):
        for copy in cache[i]:
            copy.wait()
        scores = scores_of(*group)
        if held is not None:
            mix(*held)
        held = (*group, scores)
    mix(*held)

    for copy in late:
        copy.wait()
    by_row = jnp.dot(back, mixed_rows[...], preferred_element_type=jnp.float32).astype(jnp.bfloat16)
    outs = [
        jnp.dot(
            by_row[h * rows : (h + 1) * rows], w_value_up[h], preferred_element_type=jnp.float32
        ).astype(jnp.bfloat16)
        for h in range(heads)
    ]
    partial_ref[...] = jnp.dot(
        jnp.concatenate(outs, axis=1), w_out[...], preferred_element_type=jnp.float32
    ).astype(jnp.bfloat16)


def attend_rows(
    hidden, lengths, attn_gain, latent_gain, expert_ids, route_weights,
    w_query, w_latent, w_rope_key, w_key_up, latent_cache, rope_cache, w_value_up, w_out,
):
    rows, model_width = hidden.shape
    heads, latent_width = w_key_up.shape[:2]
    capacity = rows // ROW_Q * MOST
    slot_count = EXPERTS * capacity
    sources = (
        hidden, lengths.reshape(1, rows), attn_gain.reshape(1, -1), latent_gain.reshape(1, -1),
        expert_ids.T, route_weights.T, w_query, w_key_up, w_latent, w_rope_key, w_value_up, w_out,
        latent_cache, rope_cache,
    )
    return pl.pallas_call(
        attend_kernel,
        out_shape=(
            jax.ShapeDtypeStruct((rows, model_width), jnp.bfloat16),
            jax.ShapeDtypeStruct((rows, slot_count), jnp.bfloat16),
            jax.ShapeDtypeStruct((2 * rows, slot_count), jnp.bfloat16),
        ),
        in_specs=[pl.BlockSpec(memory_space=pltpu.HBM)] * len(sources),
        out_specs=(pl.BlockSpec(memory_space=pltpu.VMEM),) * 3,
        scratch_shapes=[pltpu.VMEM(array.shape, array.dtype) for array in sources]
        + [
            pltpu.VMEM((rows * heads, latent_width), jnp.bfloat16),
            pltpu.VMEM((rows * heads, w_rope_key.shape[0]), jnp.bfloat16),
            pltpu.VMEM((rows * heads, latent_width), jnp.bfloat16),
            pltpu.SemaphoreType.DMA((12,)),
            pltpu.SemaphoreType.DMA((len(GROUPS), 2)),
        ],
        compiler_params=pltpu.CompilerParams(vmem_limit_bytes=40 << 20),
        name="attend_rows",
    )(*[pltpu.with_memory_space_constraint(array, pltpu.HBM) for array in sources])


def per_device(
    hidden,
    lengths,
    attn_gain,
    w_query,
    w_latent,
    latent_gain,
    w_rope_key,
    w_key_up,
    w_value_up,
    w_out,
    latent_cache,
    rope_cache,
    ffn_gain,
    expert_ids,
    route_weights,
    w_gate_up,
    w_down,
):
    devices = lax.axis_size("dev")
    model_width = hidden.shape[1]
    partial_value, table, mix = attend_rows(
        hidden, lengths, attn_gain, latent_gain, expert_ids, route_weights,
        w_query, w_latent, w_rope_key, w_key_up, latent_cache, rope_cache, w_value_up, w_out,
    )
    middle = (hidden.astype(jnp.float32) + section_sum(partial_value)).astype(jnp.bfloat16)
    expert_in = rms_norm(middle.astype(jnp.float32), ffn_gain).astype(jnp.bfloat16)
    capacity = table.shape[1] // EXPERTS
    packed = pack_rows(expert_in, table).reshape(devices, -1, capacity, model_width)
    partial_out = expert_part(
        lax.all_to_all(packed, "dev", split_axis=0, concat_axis=0, tiled=True), w_gate_up, w_down
    )
    returned = lax.all_to_all(
        partial_out.astype(jnp.bfloat16), "dev", split_axis=0, concat_axis=0, tiled=True
    )
    routed = section_sum(combine_rows(returned, mix).astype(jnp.bfloat16))
    return (middle.astype(jnp.float32) + routed).astype(jnp.bfloat16)


def solution(mesh):
    in_specs = (
        P("dev", None),
        P("dev"),
        P(),
        P(None, "section"),
        P(),
        P(),
        P(),
        P("section", None, None),
        P("section", None, None),
        P("section", None),
        P("dev", None, None),
        P("dev", None, None),
        P(),
        P("dev", None),
        P("dev", None),
        P("dev", None, "section", None),
        P("dev", "section", None),
    )
    out_specs = P("dev", None)
    return jax.shard_map(
        per_device, mesh=mesh, in_specs=in_specs, out_specs=out_specs, check_vma=False
    )
```

```python
import jax
import jax.numpy as jnp
from jax import lax
from jax.experimental import pallas as pl
from jax.experimental.pallas import tpu as pltpu
from jax.sharding import PartitionSpec as P

EXPERTS = 64
MOST = 2
ROW_Q = 8
GROUPS = (16, 16)
LANES = 128


epsilon = 1e-06
far_below = -1e30


def rms_norm(values, norm_gain):
    mean_square = jnp.mean(values * values, axis=-1, keepdims=True)
    return values * lax.rsqrt(mean_square + epsilon) * norm_gain


def pack_rows(source, table):
    packed = lax.dot_general(
        table, source, (((0,), (0,)), ((), ())), preferred_element_type=jnp.float32
    )
    return packed.astype(jnp.bfloat16)


def expert_kernel(rows_ref, gate_up_ref, down_ref, out_ref):
    sources, experts, capacity, width = rows_ref.shape
    contract_last = (((1,), (1,)), ((), ()))
    for e in range(experts):
        rows = rows_ref[:, e].reshape(sources * capacity, width)
        gate = lax.dot_general(
            rows, gate_up_ref[e, 0], contract_last, preferred_element_type=jnp.float32
        )
        up = lax.dot_general(
            rows, gate_up_ref[e, 1], contract_last, preferred_element_type=jnp.float32
        )
        activated = (gate / (1.0 + jnp.exp(-gate)) * up).astype(jnp.bfloat16)
        out = jnp.dot(activated, down_ref[e], preferred_element_type=jnp.float32)
        out_ref[:, e] = out.astype(jnp.bfloat16).reshape(sources, capacity, width)


def expert_part(slot_rows, w_gate_up, w_down):
    return pl.pallas_call(
        expert_kernel,
        out_shape=jax.ShapeDtypeStruct(slot_rows.shape, jnp.bfloat16),
        in_specs=[pl.BlockSpec(memory_space=pltpu.VMEM)] * 3,
        out_specs=pl.BlockSpec(memory_space=pltpu.VMEM),
        compiler_params=pltpu.CompilerParams(vmem_limit_bytes=34 << 20),
        name="expert_part",
    )(slot_rows, w_gate_up, w_down)


def section_sum(partial):
    sections = lax.axis_size("section")
    shifted = [
        lax.ppermute(partial, "section", [(i, (i + step) % sections) for i in range(sections)])
        for step in range(1, sections)
    ]
    held = [value.astype(jnp.float32) for value in [partial] + shifted]
    half = sections // 2
    pairs = [held[i] + held[i + half] for i in range(half)]
    return sum(pairs[1:], pairs[0])


def combine_rows(returned, mix):
    flat_out = returned.reshape(-1, returned.shape[-1])
    sums = jnp.dot(mix, flat_out, preferred_element_type=jnp.float32)
    half = mix.shape[0] // 2
    return sums[:half] + sums[half:]


def attend_kernel(*refs):
    sources, rest = refs[:14], refs[14:]
    partial_ref, table_ref, mix_ref = rest[:3]
    held_refs, rest = rest[3:17], rest[17:]
    query_rows, turned_rows, mixed_rows, load_sems, cache_sems = rest
    (
        hidden_ref, lengths_ref, attn_gain_ref, latent_gain_ref, ids_ref, weights_ref,
        w_query, w_key_up, w_latent, w_rope, w_value_up, w_out, latent, rope,
    ) = held_refs
    latent_hbm, rope_hbm = sources[12:]
    rows = hidden_ref.shape[0]
    heads, latent_width, nope_width = w_key_up.shape
    rope_width = w_rope.shape[0]
    slots = latent.shape[1]
    half = rope_width // 2
    head_width = nope_width + rope_width
    flat = rows * heads
    score_scale = head_width ** (-0.5)
    starts = [sum(GROUPS[:i]) for i in range(len(GROUPS))]

    loads = [
        pltpu.make_async_copy(source, target, load_sems.at[i])
        for i, (source, target) in enumerate(zip(sources[:12], held_refs[:12]))
    ]
    small, early, late = loads[:6], loads[6:10], loads[10:]
    cache = []
    for i, (first, size) in enumerate(zip(starts, GROUPS)):
        span = pl.ds(first, size)
        cache.append(
            (
                pltpu.make_async_copy(latent_hbm.at[span], latent.at[span], cache_sems.at[i, 0]),
                pltpu.make_async_copy(rope_hbm.at[span], rope.at[span], cache_sems.at[i, 1]),
            )
        )
    for copy in small + early:
        copy.start()
    for pair in cache:
        for copy in pair:
            copy.start()
    for copy in late:
        copy.start()

    def count(shape, axis):
        return lax.broadcasted_iota(jnp.int32, shape, axis)

    one, two = count((rows, rows), 0), count((rows, rows), 1)
    same = jnp.where(one == two, 1.0, 0.0)

    def column(row):
        return jnp.sum(same * row.astype(jnp.float32), axis=1, keepdims=True)

    for copy in small:
        copy.wait()
    slot_count = table_ref.shape[1]
    capacity = slot_count // EXPERTS
    slot_index = count((rows, slot_count), 1)
    slot_expert = slot_index // capacity
    slot_place = slot_index % capacity
    named = jnp.zeros((rows, slot_count), jnp.float32)
    weight = jnp.zeros((rows, slot_count), jnp.float32)
    for k in range(ids_ref.shape[0]):
        hit = column(ids_ref[k : k + 1, :]).astype(jnp.int32) == slot_expert
        named = jnp.where(hit, 1.0, named)
        weight = jnp.where(hit, column(weights_ref[k : k + 1, :]), weight)
    before = jnp.where((two < one) & (two // ROW_Q == one // ROW_Q), 1.0, 0.0)
    rank_in = jnp.dot(
        before.astype(jnp.bfloat16), named.astype(jnp.bfloat16), preferred_element_type=jnp.float32
    )
    wanted = (count((rows, slot_count), 0) // ROW_Q) * MOST + rank_in.astype(jnp.int32)
    taken = (slot_place == wanted) & (named > 0.0)
    table_ref[...] = jnp.where(taken, 1.0, 0.0).astype(jnp.bfloat16)
    weight = jnp.where(taken, weight, 0.0)
    upper = weight.astype(jnp.bfloat16)
    mix_ref[0:rows, :] = upper
    mix_ref[rows : 2 * rows, :] = (weight - upper.astype(jnp.float32)).astype(jnp.bfloat16)

    lengths = lengths_ref[...].astype(jnp.float32)
    repeat = jnp.where(count((flat, rows), 0) // heads == count((flat, rows), 1), 1.0, 0.0)
    flat_length = jnp.sum(repeat * lengths, axis=1, keepdims=True)
    row_length = column(lengths)
    repeat = repeat.astype(jnp.bfloat16)
    frequency = jnp.exp(
        -jnp.log(10000.0) * count((1, half), 1).astype(jnp.float32) / half
    )
    angles = row_length * frequency
    cosine, sine_part = jnp.cos(angles), jnp.sin(angles)

    def turned(first_half, second):
        return jnp.concatenate(
            [first_half * cosine - second * sine_part, second * cosine + first_half * sine_part],
            axis=1,
        ).astype(jnp.bfloat16)

    values = hidden_ref[...].astype(jnp.float32)
    mean_square = jnp.mean(values * values, axis=1, keepdims=True)
    normed = (values * lax.rsqrt(mean_square + epsilon) * attn_gain_ref[...]).astype(jnp.bfloat16)

    early[0].wait()
    queries = jnp.dot(normed, w_query[...], preferred_element_type=jnp.float32).astype(jnp.bfloat16)
    early[1].wait()
    def wide(ref, span):
        return jnp.concatenate([ref[c, span, :] for c in range(latent_width // LANES)], axis=1)

    for h in range(heads):
        start = h * head_width
        own_rows = pl.ds(h, rows, stride=heads)
        middle = start + nope_width
        in_latent = lax.dot_general(
            queries[:, start : start + nope_width], w_key_up[h], (((1,), (1,)), ((), ())),
            preferred_element_type=jnp.float32,
        )
        for c in range(latent_width // LANES):
            query_rows[c, own_rows, :] = in_latent[:, c * LANES : (c + 1) * LANES]
        in_rope = turned(
            queries[:, middle : middle + half].astype(jnp.float32),
            queries[:, middle + half : middle + rope_width].astype(jnp.float32),
        ).astype(jnp.float32)
        turned_rows[own_rows, :] = jnp.concatenate([in_rope, in_rope], axis=1)

    early[2].wait()
    latent_raw = jnp.dot(normed, w_latent[...], preferred_element_type=jnp.float32)
    mean_square = jnp.mean(latent_raw * latent_raw, axis=1, keepdims=True)
    latent_new = (latent_raw * lax.rsqrt(mean_square + epsilon) * latent_gain_ref[...]).astype(
        jnp.bfloat16
    )
    early[3].wait()
    key_raw = lax.dot_general(
        normed, w_rope[...], (((1,), (1,)), ((), ())), preferred_element_type=jnp.float32
    )
    key_new = turned(key_raw[:, :half], key_raw[:, half:])
    latent_flat = jnp.dot(repeat, latent_new, preferred_element_type=jnp.float32)
    key_flat = jnp.dot(repeat, key_new, preferred_element_type=jnp.float32)
    self_score = (
        jnp.sum(wide(query_rows, slice(0, flat)).astype(jnp.bfloat16).astype(jnp.float32) * latent_flat, axis=1, keepdims=True)
        + jnp.sum(turned_rows[:, 0:rope_width] * key_flat, axis=1, keepdims=True)
    ) * score_scale

    def scores_of(first, size):
        tile = size * heads
        span = slice(first * heads, first * heads + tile)
        query = wide(query_rows, span).astype(jnp.bfloat16)
        query_turned = turned_rows[span, 0:rope_width].astype(jnp.bfloat16)
        owner = count((tile, 1), 0) // heads
        lane_owner = count((1, tile), 1) // heads
        total = jnp.zeros((tile, slots), jnp.float32)
        pieces = []
        for j in range(size):
            low = j // 4 * 16
            part = lax.dot_general(
                query[low : low + 16], latent[first + j], (((1,), (1,)), ((), ())),
                preferred_element_type=jnp.float32,
            ) + jnp.dot(query_turned[low : low + 16], rope[first + j], preferred_element_type=jnp.float32)
            near = jnp.where(owner[:16] == j % 4, part, near) if j % 4 else part
            if j % 4 == 3:
                pieces.append(near)
        return jnp.concatenate(pieces, axis=0) * score_scale

    def mix(first, size, scores):
        tile = size * heads
        span = slice(first * heads, first * heads + tile)
        valid = count((tile, slots), 1).astype(jnp.float32) < flat_length[span]
        own = self_score[span]
        masked = jnp.where(valid, scores, far_below)
        peak = jnp.maximum(jnp.max(masked, axis=1, keepdims=True), own)
        weights = jnp.where(valid, jnp.exp(masked - peak), 0.0)
        self_weight = jnp.exp(own - peak)
        total = jnp.sum(weights, axis=1, keepdims=True) + self_weight
        probs = (weights / total).astype(jnp.bfloat16)
        prob_self = (self_weight / total).astype(jnp.bfloat16).astype(jnp.float32)
        owner = count((tile, 1), 0) // heads
        pieces = []
        for j in range(size):
            low = j // 4 * 16
            part = jnp.dot(probs[low : low + 16], latent[first + j], preferred_element_type=jnp.float32)
            near = jnp.where(owner[:16] == j % 4, part, near) if j % 4 else part
            if j % 4 == 3:
                pieces.append(near)
        mixed = jnp.concatenate(pieces, axis=0)
        mixed = mixed + prob_self * latent_flat[span]
        for c in range(latent_width // LANES):
            mixed_rows[c, span, :] = mixed[:, c * LANES : (c + 1) * LANES]

    held = None
    for i, group in enumerate(zip(starts, GROUPS)):
        for copy in cache[i]:
            copy.wait()
        scores = scores_of(*group)
        if held is not None:
            mix(*held)
        held = (*group, scores)
    mix(*held)

    for copy in late:
        copy.wait()
    outs = [
        jnp.dot(
            wide(mixed_rows, pl.ds(h, rows, stride=heads)).astype(jnp.bfloat16), w_value_up[h],
            preferred_element_type=jnp.float32,
        ).astype(jnp.bfloat16)
        for h in range(heads)
    ]
    partial_ref[...] = jnp.dot(
        jnp.concatenate(outs, axis=1), w_out[...], preferred_element_type=jnp.float32
    ).astype(jnp.bfloat16)


def attend_rows(
    hidden, lengths, attn_gain, latent_gain, expert_ids, route_weights,
    w_query, w_latent, w_rope_key, w_key_up, latent_cache, rope_cache, w_value_up, w_out,
):
    rows, model_width = hidden.shape
    heads, latent_width = w_key_up.shape[:2]
    capacity = rows // ROW_Q * MOST
    slot_count = EXPERTS * capacity
    sources = (
        hidden, lengths.reshape(1, rows), attn_gain.reshape(1, -1), latent_gain.reshape(1, -1),
        expert_ids.T, route_weights.T, w_query, w_key_up, w_latent, w_rope_key, w_value_up, w_out,
        latent_cache, rope_cache,
    )
    return pl.pallas_call(
        attend_kernel,
        out_shape=(
            jax.ShapeDtypeStruct((rows, model_width), jnp.bfloat16),
            jax.ShapeDtypeStruct((rows, slot_count), jnp.bfloat16),
            jax.ShapeDtypeStruct((2 * rows, slot_count), jnp.bfloat16),
        ),
        in_specs=[pl.BlockSpec(memory_space=pltpu.HBM)] * len(sources),
        out_specs=(pl.BlockSpec(memory_space=pltpu.VMEM),) * 3,
        scratch_shapes=[pltpu.VMEM(array.shape, array.dtype) for array in sources]
        + [
            pltpu.VMEM((latent_width // LANES, rows * heads, LANES), jnp.float32),
            pltpu.VMEM((rows * heads, LANES), jnp.float32),
            pltpu.VMEM((latent_width // LANES, rows * heads, LANES), jnp.float32),
            pltpu.SemaphoreType.DMA((12,)),
            pltpu.SemaphoreType.DMA((len(GROUPS), 2)),
        ],
        compiler_params=pltpu.CompilerParams(vmem_limit_bytes=40 << 20),
        name="attend_rows",
    )(*[pltpu.with_memory_space_constraint(array, pltpu.HBM) for array in sources])


def per_device(
    hidden,
    lengths,
    attn_gain,
    w_query,
    w_latent,
    latent_gain,
    w_rope_key,
    w_key_up,
    w_value_up,
    w_out,
    latent_cache,
    rope_cache,
    ffn_gain,
    expert_ids,
    route_weights,
    w_gate_up,
    w_down,
):
    devices = lax.axis_size("dev")
    model_width = hidden.shape[1]
    partial_value, table, mix = attend_rows(
        hidden, lengths, attn_gain, latent_gain, expert_ids, route_weights,
        w_query, w_latent, w_rope_key, w_key_up, latent_cache, rope_cache, w_value_up, w_out,
    )
    middle = (hidden.astype(jnp.float32) + section_sum(partial_value)).astype(jnp.bfloat16)
    expert_in = rms_norm(middle.astype(jnp.float32), ffn_gain).astype(jnp.bfloat16)
    capacity = table.shape[1] // EXPERTS
    packed = pack_rows(expert_in, table).reshape(devices, -1, capacity, model_width)
    partial_out = expert_part(
        lax.all_to_all(packed, "dev", split_axis=0, concat_axis=0, tiled=True), w_gate_up, w_down
    )
    returned = lax.all_to_all(
        partial_out, "dev", split_axis=0, concat_axis=0, tiled=True
    )
    routed = section_sum(combine_rows(returned, mix).astype(jnp.bfloat16))
    return (middle.astype(jnp.float32) + routed).astype(jnp.bfloat16)


def solution(mesh):
    in_specs = (
        P("dev", None),
        P("dev"),
        P(),
        P(None, "section"),
        P(),
        P(),
        P(),
        P("section", None, None),
        P("section", None, None),
        P("section", None),
        P("dev", None, None),
        P("dev", None, None),
        P(),
        P("dev", None),
        P("dev", None),
        P("dev", None, "section", None),
        P("dev", "section", None),
    )
    out_specs = P("dev", None)
    return jax.shard_map(
        per_device, mesh=mesh, in_specs=in_specs, out_specs=out_specs, check_vma=False
    )
```

```python
import jax
import jax.numpy as jnp
from jax import lax
from jax.experimental import pallas as pl
from jax.experimental.pallas import tpu as pltpu
from jax.sharding import PartitionSpec as P

EXPERTS = 64
MOST = 2
ROW_Q = 8
GROUPS = (16, 16)
LANES = 128


epsilon = 1e-06
far_below = -1e30


def rms_norm(values, norm_gain):
    mean_square = jnp.mean(values * values, axis=-1, keepdims=True)
    return values * lax.rsqrt(mean_square + epsilon) * norm_gain


def pack_rows(source, table):
    packed = lax.dot_general(
        table, source, (((0,), (0,)), ((), ())), preferred_element_type=jnp.float32
    )
    return packed.astype(jnp.bfloat16)


def expert_kernel(rows_ref, gate_up_ref, down_ref, out_ref):
    sources, experts, capacity, width = rows_ref.shape
    contract_last = (((1,), (1,)), ((), ()))
    activated = []
    for e in range(experts):
        rows = rows_ref[:, e].reshape(sources * capacity, width)
        gate = lax.dot_general(
            gate_up_ref[e, 0], rows, contract_last, preferred_element_type=jnp.float32
        )
        up = lax.dot_general(
            gate_up_ref[e, 1], rows, contract_last, preferred_element_type=jnp.float32
        )
        activated.append((gate / (1.0 + jnp.exp(-gate)) * up).astype(jnp.bfloat16).T)
    half = width // 2
    for e in range(experts):
        for start in (0, half):
            span = slice(start, start + half)
            out = jnp.dot(activated[e], down_ref[e, :, span], preferred_element_type=jnp.float32)
            out_ref[:, e, :, span] = out.astype(jnp.bfloat16).reshape(sources, capacity, half)


def expert_part(slot_rows, w_gate_up, w_down):
    return pl.pallas_call(
        expert_kernel,
        out_shape=jax.ShapeDtypeStruct(slot_rows.shape, jnp.bfloat16),
        in_specs=[pl.BlockSpec(memory_space=pltpu.VMEM)] * 3,
        out_specs=pl.BlockSpec(memory_space=pltpu.VMEM),
        compiler_params=pltpu.CompilerParams(vmem_limit_bytes=34 << 20),
        name="expert_part",
    )(slot_rows, w_gate_up, w_down)


def section_sum(partial):
    sections = lax.axis_size("section")
    shifted = [
        lax.ppermute(partial, "section", [(i, (i + step) % sections) for i in range(sections)])
        for step in range(1, sections)
    ]
    held = [value.astype(jnp.float32) for value in [partial] + shifted]
    half = sections // 2
    pairs = [held[i] + held[i + half] for i in range(half)]
    return sum(pairs[1:], pairs[0])


def combine_rows(returned, mix):
    flat_out = returned.reshape(-1, returned.shape[-1])
    sums = jnp.dot(mix, flat_out, preferred_element_type=jnp.float32)
    half = mix.shape[0] // 2
    return sums[:half] + sums[half:]


def attend_kernel(*refs):
    sources, rest = refs[:14], refs[14:]
    partial_ref, table_ref, mix_ref = rest[:3]
    held_refs, rest = rest[3:17], rest[17:]
    query_rows, turned_rows, mixed_rows, load_sems, cache_sems = rest
    (
        hidden_ref, lengths_ref, attn_gain_ref, latent_gain_ref, ids_ref, weights_ref,
        w_query, w_key_up, w_latent, w_rope, w_value_up, w_out, latent, rope,
    ) = held_refs
    latent_hbm, rope_hbm = sources[12:]
    rows = hidden_ref.shape[0]
    heads, latent_width, nope_width = w_key_up.shape
    rope_width = w_rope.shape[0]
    slots = latent.shape[1]
    half = rope_width // 2
    head_width = nope_width + rope_width
    flat = rows * heads
    score_scale = head_width ** (-0.5)
    starts = [sum(GROUPS[:i]) for i in range(len(GROUPS))]

    loads = [
        pltpu.make_async_copy(source, target, load_sems.at[i])
        for i, (source, target) in enumerate(zip(sources[:12], held_refs[:12]))
    ]
    small, early, late = loads[:6], loads[6:10], loads[10:]
    cache = []
    for i, (first, size) in enumerate(zip(starts, GROUPS)):
        span = pl.ds(first, size)
        cache.append(
            (
                pltpu.make_async_copy(latent_hbm.at[span], latent.at[span], cache_sems.at[i, 0]),
                pltpu.make_async_copy(rope_hbm.at[span], rope.at[span], cache_sems.at[i, 1]),
            )
        )
    for copy in small + early:
        copy.start()
    for pair in cache:
        for copy in pair:
            copy.start()
    for copy in late:
        copy.start()

    def count(shape, axis):
        return lax.broadcasted_iota(jnp.int32, shape, axis)

    one, two = count((rows, rows), 0), count((rows, rows), 1)
    same = jnp.where(one == two, 1.0, 0.0)

    def column(row):
        return jnp.sum(same * row.astype(jnp.float32), axis=1, keepdims=True)

    for copy in small:
        copy.wait()
    slot_count = table_ref.shape[1]
    capacity = slot_count // EXPERTS
    slot_index = count((rows, slot_count), 1)
    slot_expert = slot_index // capacity
    slot_place = slot_index % capacity
    named = jnp.zeros((rows, slot_count), jnp.float32)
    weight = jnp.zeros((rows, slot_count), jnp.float32)
    for k in range(ids_ref.shape[0]):
        hit = column(ids_ref[k : k + 1, :]).astype(jnp.int32) == slot_expert
        named = jnp.where(hit, 1.0, named)
        weight = jnp.where(hit, column(weights_ref[k : k + 1, :]), weight)
    before = jnp.where((two < one) & (two // ROW_Q == one // ROW_Q), 1.0, 0.0)
    rank_in = jnp.dot(
        before.astype(jnp.bfloat16), named.astype(jnp.bfloat16), preferred_element_type=jnp.float32
    )
    wanted = (count((rows, slot_count), 0) // ROW_Q) * MOST + rank_in.astype(jnp.int32)
    taken = (slot_place == wanted) & (named > 0.0)
    table_ref[...] = jnp.where(taken, 1.0, 0.0).astype(jnp.bfloat16)
    weight = jnp.where(taken, weight, 0.0)
    upper = weight.astype(jnp.bfloat16)
    mix_ref[0:rows, :] = upper
    mix_ref[rows : 2 * rows, :] = (weight - upper.astype(jnp.float32)).astype(jnp.bfloat16)

    lengths = lengths_ref[...].astype(jnp.float32)
    repeat = jnp.where(count((flat, rows), 0) // heads == count((flat, rows), 1), 1.0, 0.0)
    flat_length = jnp.sum(repeat * lengths, axis=1, keepdims=True)
    row_length = column(lengths)
    repeat = repeat.astype(jnp.bfloat16)
    frequency = jnp.exp(
        -jnp.log(10000.0) * count((1, half), 1).astype(jnp.float32) / half
    )
    angles = row_length * frequency
    cosine, sine_part = jnp.cos(angles), jnp.sin(angles)

    def turned(first_half, second):
        return jnp.concatenate(
            [first_half * cosine - second * sine_part, second * cosine + first_half * sine_part],
            axis=1,
        ).astype(jnp.bfloat16)

    values = hidden_ref[...].astype(jnp.float32)
    mean_square = jnp.mean(values * values, axis=1, keepdims=True)
    normed = (values * lax.rsqrt(mean_square + epsilon) * attn_gain_ref[...]).astype(jnp.bfloat16)

    early[0].wait()
    queries = jnp.dot(normed, w_query[...], preferred_element_type=jnp.float32).astype(jnp.bfloat16)
    early[1].wait()
    def wide(ref, span):
        return jnp.concatenate([ref[c, span, :] for c in range(latent_width // LANES)], axis=1)

    for h in range(heads):
        start = h * head_width
        own_rows = pl.ds(h, rows, stride=heads)
        middle = start + nope_width
        in_latent = lax.dot_general(
            queries[:, start : start + nope_width], w_key_up[h], (((1,), (1,)), ((), ())),
            preferred_element_type=jnp.float32,
        )
        for c in range(latent_width // LANES):
            query_rows[c, own_rows, :] = in_latent[:, c * LANES : (c + 1) * LANES]
        in_rope = turned(
            queries[:, middle : middle + half].astype(jnp.float32),
            queries[:, middle + half : middle + rope_width].astype(jnp.float32),
        ).astype(jnp.float32)
        turned_rows[own_rows, :] = jnp.concatenate([in_rope, in_rope], axis=1)

    early[2].wait()
    latent_raw = jnp.dot(normed, w_latent[...], preferred_element_type=jnp.float32)
    mean_square = jnp.mean(latent_raw * latent_raw, axis=1, keepdims=True)
    latent_new = (latent_raw * lax.rsqrt(mean_square + epsilon) * latent_gain_ref[...]).astype(
        jnp.bfloat16
    )
    early[3].wait()
    key_raw = lax.dot_general(
        normed, w_rope[...], (((1,), (1,)), ((), ())), preferred_element_type=jnp.float32
    )
    key_new = turned(key_raw[:, :half], key_raw[:, half:])
    latent_flat = jnp.dot(repeat, latent_new, preferred_element_type=jnp.float32)
    key_flat = jnp.dot(repeat, key_new, preferred_element_type=jnp.float32)
    self_score = (
        jnp.sum(wide(query_rows, slice(0, flat)).astype(jnp.bfloat16).astype(jnp.float32) * latent_flat, axis=1, keepdims=True)
        + jnp.sum(turned_rows[:, 0:rope_width] * key_flat, axis=1, keepdims=True)
    ) * score_scale

    def scores_of(first, size):
        tile = size * heads
        span = slice(first * heads, first * heads + tile)
        query = wide(query_rows, span).astype(jnp.bfloat16)
        query_turned = turned_rows[span, 0:rope_width].astype(jnp.bfloat16)
        owner = count((tile, 1), 0) // heads
        lane_owner = count((1, tile), 1) // heads
        total = jnp.zeros((tile, slots), jnp.float32)
        pieces = []
        for j in range(size):
            low = j // 4 * 16
            part = lax.dot_general(
                query[low : low + 16], latent[first + j], (((1,), (1,)), ((), ())),
                preferred_element_type=jnp.float32,
            ) + jnp.dot(query_turned[low : low + 16], rope[first + j], preferred_element_type=jnp.float32)
            near = jnp.where(owner[:16] == j % 4, part, near) if j % 4 else part
            if j % 4 == 3:
                pieces.append(near)
        return jnp.concatenate(pieces, axis=0) * score_scale

    def mix(first, size, scores):
        tile = size * heads
        span = slice(first * heads, first * heads + tile)
        valid = count((tile, slots), 1).astype(jnp.float32) < flat_length[span]
        own = self_score[span]
        masked = jnp.where(valid, scores, far_below)
        peak = jnp.maximum(jnp.max(masked, axis=1, keepdims=True), own)
        weights = jnp.where(valid, jnp.exp(masked - peak), 0.0)
        self_weight = jnp.exp(own - peak)
        total = jnp.sum(weights, axis=1, keepdims=True) + self_weight
        probs = (weights / total).astype(jnp.bfloat16)
        prob_self = (self_weight / total).astype(jnp.bfloat16).astype(jnp.float32)
        owner = count((tile, 1), 0) // heads
        pieces = []
        for j in range(size):
            low = j // 4 * 16
            part = jnp.dot(probs[low : low + 16], latent[first + j], preferred_element_type=jnp.float32)
            near = jnp.where(owner[:16] == j % 4, part, near) if j % 4 else part
            if j % 4 == 3:
                pieces.append(near)
        mixed = jnp.concatenate(pieces, axis=0)
        mixed = mixed + prob_self * latent_flat[span]
        for c in range(latent_width // LANES):
            mixed_rows[c, span, :] = mixed[:, c * LANES : (c + 1) * LANES]

    held = None
    for i, group in enumerate(zip(starts, GROUPS)):
        for copy in cache[i]:
            copy.wait()
        scores = scores_of(*group)
        if held is not None:
            mix(*held)
        held = (*group, scores)
    mix(*held)

    for copy in late:
        copy.wait()
    outs = [
        jnp.dot(
            wide(mixed_rows, pl.ds(h, rows, stride=heads)).astype(jnp.bfloat16), w_value_up[h],
            preferred_element_type=jnp.float32,
        ).astype(jnp.bfloat16)
        for h in range(heads)
    ]
    partial_ref[...] = jnp.dot(
        jnp.concatenate(outs, axis=1), w_out[...], preferred_element_type=jnp.float32
    ).astype(jnp.bfloat16)


def attend_rows(
    hidden, lengths, attn_gain, latent_gain, expert_ids, route_weights,
    w_query, w_latent, w_rope_key, w_key_up, latent_cache, rope_cache, w_value_up, w_out,
):
    rows, model_width = hidden.shape
    heads, latent_width = w_key_up.shape[:2]
    capacity = rows // ROW_Q * MOST
    slot_count = EXPERTS * capacity
    sources = (
        hidden, lengths.reshape(1, rows), attn_gain.reshape(1, -1), latent_gain.reshape(1, -1),
        expert_ids.T, route_weights.T, w_query, w_key_up, w_latent, w_rope_key, w_value_up, w_out,
        latent_cache, rope_cache,
    )
    return pl.pallas_call(
        attend_kernel,
        out_shape=(
            jax.ShapeDtypeStruct((rows, model_width), jnp.bfloat16),
            jax.ShapeDtypeStruct((rows, slot_count), jnp.bfloat16),
            jax.ShapeDtypeStruct((2 * rows, slot_count), jnp.bfloat16),
        ),
        in_specs=[pl.BlockSpec(memory_space=pltpu.HBM)] * len(sources),
        out_specs=(pl.BlockSpec(memory_space=pltpu.VMEM),) * 3,
        scratch_shapes=[pltpu.VMEM(array.shape, array.dtype) for array in sources]
        + [
            pltpu.VMEM((latent_width // LANES, rows * heads, LANES), jnp.float32),
            pltpu.VMEM((rows * heads, LANES), jnp.float32),
            pltpu.VMEM((latent_width // LANES, rows * heads, LANES), jnp.float32),
            pltpu.SemaphoreType.DMA((12,)),
            pltpu.SemaphoreType.DMA((len(GROUPS), 2)),
        ],
        compiler_params=pltpu.CompilerParams(vmem_limit_bytes=40 << 20),
        name="attend_rows",
    )(*[pltpu.with_memory_space_constraint(array, pltpu.HBM) for array in sources])


def per_device(
    hidden,
    lengths,
    attn_gain,
    w_query,
    w_latent,
    latent_gain,
    w_rope_key,
    w_key_up,
    w_value_up,
    w_out,
    latent_cache,
    rope_cache,
    ffn_gain,
    expert_ids,
    route_weights,
    w_gate_up,
    w_down,
):
    devices = lax.axis_size("dev")
    model_width = hidden.shape[1]
    partial_value, table, mix = attend_rows(
        hidden, lengths, attn_gain, latent_gain, expert_ids, route_weights,
        w_query, w_latent, w_rope_key, w_key_up, latent_cache, rope_cache, w_value_up, w_out,
    )
    middle = (hidden.astype(jnp.float32) + section_sum(partial_value)).astype(jnp.bfloat16)
    expert_in = rms_norm(middle.astype(jnp.float32), ffn_gain).astype(jnp.bfloat16)
    capacity = table.shape[1] // EXPERTS
    packed = pack_rows(expert_in, table).reshape(devices, -1, capacity, model_width)
    partial_out = expert_part(
        lax.all_to_all(packed, "dev", split_axis=0, concat_axis=0, tiled=True), w_gate_up, w_down
    )
    returned = lax.all_to_all(
        partial_out, "dev", split_axis=0, concat_axis=0, tiled=True
    )
    routed = section_sum(combine_rows(returned, mix).astype(jnp.bfloat16))
    return (middle.astype(jnp.float32) + routed).astype(jnp.bfloat16)


def solution(mesh):
    in_specs = (
        P("dev", None),
        P("dev"),
        P(),
        P(None, "section"),
        P(),
        P(),
        P(),
        P("section", None, None),
        P("section", None, None),
        P("section", None),
        P("dev", None, None),
        P("dev", None, None),
        P(),
        P("dev", None),
        P("dev", None),
        P("dev", None, "section", None),
        P("dev", "section", None),
    )
    out_specs = P("dev", None)
    return jax.shard_map(
        per_device, mesh=mesh, in_specs=in_specs, out_specs=out_specs, check_vma=False
    )
```
